256 devices in a mesh: gx: 16 (over x, z_lo, core), gy: 16 (over z_hi, y).
Axes of the slice: x: 4, y: 4, z: 8 (z_hi: 4, z_lo: 2; z = z_hi * 2 + z_lo), core: 2. Of those that a mesh axis runs over, the one named last changes fastest.
Arguments:
- farm_velocity: float32 [3, 256, 128, 192], P(None, 'gx', 'gy'), may hold values from -6 to 6
- precursor_velocity: float32 [3, 256, 128, 192], P(None, 'gx', 'gy'), may hold values from -6 to 6
- turb_cell: int32 [16, 16, 256], P('gx', 'gy'), may hold values from 0 to 24575
- turb_slot: int32 [16, 16, 256], P('gx', 'gy'), may hold values from 0 to 15
- disk_mask: int32 [16, 16, 256], P('gx', 'gy'), may hold values 0 or 1
Outputs:
- farm_new: float32 [3, 256, 128, 192], P(None, 'gx', 'gy')
- precursor_new: float32 [3, 256, 128, 192], P(None, 'gx', 'gy')
The draws below stay inside these ranges and needn't reach their ends.
Inputs may be any that keep to these rules, and one draw needn't show every extreme that they name: `turb_cell`: the cell is (x * 8 + y) * 192 + z within the device's tile of 16 x 8 x 192 cells.
All inputs are finite; a program needn't handle non-finite values. No bound on the sum of `disk_mask` on one device may be relied on, other than what follows from the above.
Results may differ from the reference program's by a relative error of at most 0.0003.
Values sent between devices are 32-bit elements; how exact they have to be, the bound alone decides.
No kernel may reach another device: no remote copies, remote signals or barrier semaphores. Data moves between devices by JAX's collectives and lax.ppermute only.
A program may use at most 64 MiB of HBM per device.

```python
import math
import jax
import jax.numpy as jnp
from jax import lax

CX = 16
CY = 8
NZ = 192
NF = 48
TURB = 16
SLOTS = 256
NX = 256
NY = 128
N_GX = 16
N_GY = 16


def plant(values, own_key, smallest, top_value):
    longest = values.shape.index(max(values.shape))
    spots = []
    for shift in (0, 1):
        where = [jax.random.randint(jax.random.fold_in(own_key, axis), (), 0, length) for axis, length in enumerate(values.shape)]
        where[longest] = (where[longest] + shift) % values.shape[longest]
        spots.append(tuple(where))
    return values.at[spots[0]].set(smallest).at[spots[1]].set(top_value)


def levels(stream_key, shape, split, low, top_value):
    def one(position, parts):
        steps = jax.random.uniform(jax.random.fold_in(jax.random.fold_in(stream_key, 6), position), (parts,), jnp.float32, low / len(split), top_value / len(split))
        return jnp.repeat(jnp.exp(steps), shape[position] // parts).reshape((-1,) + (1,) * (len(shape) - position - 1))

    level = one(*split[0])
    for cut in split[1:]:
        level = level * one(*cut)
    return level


def noise(key, shape, spread, most, split=(), held_as=jnp.bfloat16):
    values = jax.random.normal(key, shape, jnp.float32) * spread
    if len(split) > 0:
        values = levels(key, shape, split, -0.22, 0.18) * values
    return jnp.clip(values, min=-most, max=most).astype(held_as)


def setup_inputs(seed: int = 0) -> dict:
    key_list = jax.random.split(jax.random.key(seed), 6)
    return {
        "farm_velocity": noise(key_list[0], (3, NX, NY, NZ), 1.0, 6.0, ((1, 16), (2, 16)), jnp.float32),
        "precursor_velocity": noise(key_list[1], (3, NX, NY, NZ), 1.0, 6.0, ((1, 16), (2, 16)), jnp.float32),
        "turb_cell": plant(jax.random.randint(key_list[2], (N_GX, N_GY, SLOTS), 0, CX * CY * NZ), jax.random.fold_in(key_list[2], 1), 0, (CX * CY * NZ) - 1).astype(jnp.int32),
        "turb_slot": plant(jax.random.randint(key_list[3], (N_GX, N_GY, SLOTS), 0, TURB), jax.random.fold_in(key_list[3], 1), 0, TURB - 1).astype(jnp.int32),
        "disk_mask": plant((jax.random.randint(key_list[4], (N_GX, N_GY, SLOTS), 0, 4) < 1).astype(jnp.int32), jax.random.fold_in(key_list[4], 1), 0, 1),
    }


WIND = 3.0
STEP = 0.1
SMAG = 0.0289
THRUST = 1.33
DIFFUSE = 0.05
HIGH = lax.Precision.HIGHEST

def inner(arr, axis, start, length):
    out = arr
    for dim in range(3):
        place = out.ndim - 3 + dim
        extent = arr.shape[arr.ndim - 3 + dim]
        if dim == axis:
            out = lax.slice_in_dim(out, start, start + length, axis=place)
        else:
            out = lax.slice_in_dim(out, 1, extent - 1, axis=place)
    return out

def farm_tendency(ext):
    padded = jnp.pad(ext, ((0, 0), (0, 0), (0, 0), (2, 2)))
    cycle = padded[:, 1:-1, 1:-1, 1:-1]
    grads = []
    for axis in range(3):
        extent = padded.shape[1 + axis]
        grads.append(0.5 * (inner(padded, axis, 2, extent - 2) - inner(padded, axis, 0, extent - 2)))
    square = jnp.zeros(cycle.shape[1:], jnp.float32)
    for first in range(3):
        for second in range(3):
            strain = 0.5 * (grads[second][first] + grads[first][second])
            square = square + strain * strain
    eddy = SMAG * jnp.sqrt(2.0 * square)
    advect = cycle + jnp.array([WIND, 0.0, 0.0], jnp.float32)[:, None, None, None]
    total = jnp.zeros((3,) + tuple((n - 2 for n in cycle.shape[1:])), jnp.float32)
    for axis in range(3):
        extent = cycle.shape[1 + axis]
        low_f = inner(cycle, axis, 0, extent - 1)
        high_f = inner(cycle, axis, 1, extent - 1)
        low_v = inner(advect[axis], axis, 0, extent - 1)
        high_v = inner(advect[axis], axis, 1, extent - 1)
        low_e = inner(eddy, axis, 0, extent - 1)
        high_e = inner(eddy, axis, 1, extent - 1)
        flux = 0.25 * (low_v + high_v) * (low_f + high_f) - 0.5 * (low_e + high_e) * (high_f - low_f)
        faces = extent - 1
        change = lax.slice_in_dim(flux, 1, faces, axis=1 + axis) - lax.slice_in_dim(flux, 0, faces - 1, axis=1 + axis)
        total = total - change
    return total

def drag_tile(flat, cells, slots, live):
    values = flat[cells] + WIND
    onehot = jnp.where((slots[:, None] == jnp.arange(TURB, dtype=jnp.int32)[None, :]) & (live[:, None] == 1), 1.0, 0.0).astype(jnp.float32)
    sums = jnp.dot(values, onehot, precision=HIGH)
    counts = lax.optimization_barrier(jnp.sum(onehot, axis=0))
    mean = sums / jnp.maximum(counts, 1.0)
    thrust = -0.5 * THRUST * mean * jnp.abs(mean)
    per_slot = jnp.dot(onehot, thrust, precision=HIGH)
    return jnp.zeros(flat.shape, jnp.float32).at[cells].add(per_slot)

def farm_rate(field, cells, slots, live):
    padded = jnp.pad(field, ((0, 0), (2, 2), (2, 2), (0, 0)), mode='wrap')

    def tile_rate(index):
        block = lax.dynamic_slice_in_dim(padded, index * CX, CX + 4, axis=1)
        return farm_tendency(block)
    rates = lax.map(tile_rate, jnp.arange(N_GX, dtype=jnp.int32))
    rates = jnp.moveaxis(rates, 0, 1).reshape(3, NX, NY, NZ)
    tiles = field[0].reshape(N_GX, CX, N_GY, CY, NZ).transpose(0, 2, 1, 3, 4).reshape(N_GX, N_GY, CX * CY * NZ)
    forces = jax.vmap(jax.vmap(drag_tile))(tiles, cells, slots, live)
    forces = forces.reshape(N_GX, N_GY, CX, CY, NZ).transpose(0, 2, 1, 3, 4).reshape(NX, NY, NZ)
    return rates.at[0].add(forces)

def precursor_step(field):
    component = jnp.arange(3)[:, None, None, None]
    height = jnp.arange(NZ)[None, None, None, :]
    field = jnp.where((component == 2) & (height == NZ - 1), 0.0, field)
    spec = jnp.fft.rfft(field, axis=1)[:, :NX // 2]
    spec = jnp.fft.fft(spec, axis=2)
    yindex = jnp.arange(NY)
    spec = jnp.where((yindex == NY // 2)[None, None, :, None], 0.0, spec)
    kx = 2.0 * math.pi / NX * jnp.arange(NX // 2).astype(jnp.float32)
    ky = 2.0 * math.pi / NY * jnp.where(yindex < NY // 2, yindex, yindex - NY).astype(jnp.float32)
    kx = kx[:, None, None]
    ky = ky[None, :, None]
    hor = kx * kx + ky * ky
    u_hat, v_hat, w_hat = (spec[0], spec[1], spec[2])
    below = w_hat - jnp.pad(w_hat, ((0, 0), (0, 0), (1, 0)))[:, :, :-1]
    div = 1j * kx * u_hat + 1j * ky * v_hat + below
    level = jnp.arange(NZ)
    ends = jnp.where((level == 0) | (level == NZ - 1), -1.0, -2.0).astype(jnp.float32)
    pin = jnp.where((hor == 0.0) & (level == 0)[None, None, :], -1.0, 0.0).astype(jnp.float32)
    diag = ends[None, None, :] - hor + pin
    lower = jnp.broadcast_to(jnp.where(level == 0, 0.0, 1.0).astype(jnp.float32), diag.shape)
    upper = jnp.broadcast_to(jnp.where(level == NZ - 1, 0.0, 1.0).astype(jnp.float32), diag.shape)
    rhs = jnp.stack([jnp.real(div), jnp.imag(div)], axis=-1)
    solved = lax.linalg.tridiagonal_solve(lower, diag, upper, rhs)
    press = solved[..., 0] + 1j * solved[..., 1]
    grad = jnp.pad(press, ((0, 0), (0, 0), (0, 1)))[:, :, 1:] - press
    grad = jnp.where((level == NZ - 1)[None, None, :], 0.0, grad)
    decay = jnp.exp(-DIFFUSE * hor)
    u_hat = (u_hat - 1j * kx * press) * decay
    v_hat = (v_hat - 1j * ky * press) * decay
    w_hat = (w_hat - grad) * decay
    spec = jnp.stack([u_hat, v_hat, w_hat])
    spec = jnp.fft.ifft(spec, axis=2)
    spec = jnp.pad(spec, ((0, 0), (0, 1), (0, 0), (0, 0)))
    return jnp.fft.irfft(spec, n=NX, axis=1).astype(jnp.float32)

def reference(farm_velocity, precursor_velocity, turb_cell, turb_slot, disk_mask):
    precursor_new = precursor_step(precursor_velocity)
    state = farm_velocity.at[:, :NF].set(precursor_new[:, NX - NF:])
    section_one = state + STEP * farm_rate(state, turb_cell, turb_slot, disk_mask)
    section_two = 0.75 * state + 0.25 * (section_one + STEP * farm_rate(section_one, turb_cell, turb_slot, disk_mask))
    farm_new = state / 3.0 + 2.0 / 3.0 * (section_two + STEP * farm_rate(section_two, turb_cell, turb_slot, disk_mask))
    return (farm_new, precursor_new)
```

```python
import functools
import math

import jax
import jax.numpy as jnp
import ml_dtypes
import numpy as np
from jax import lax
from jax.experimental import pallas as pl
from jax.experimental.pallas import tpu as pltpu
from jax.sharding import PartitionSpec as P

NF = 48
TURB = 16
WIND = 3.0
STEP = 0.1
SMAG = 0.0289
THRUST = 1.33
DIFFUSE = 0.05

CX, CY, NZ = 16, 8, 192
NX, NY = 256, 128
ROWS, COLS = 16, 16
SLOTS = 256
FRINGE = NF // CX
LANES = 256

BF = jnp.bfloat16
F32 = jnp.float32


def split(table):
    table = np.asarray(table, np.float64)
    high = table.astype(np.float32).astype(ml_dtypes.bfloat16)
    low = (table - high.astype(np.float64)).astype(np.float32).astype(ml_dtypes.bfloat16)
    return np.stack([high, low])


def vertical_tables():
    height = np.arange(NZ)[None, :]
    order = np.arange(NZ)[:, None]
    scale = np.where(order == 0, math.sqrt(1.0 / NZ), math.sqrt(2.0 / NZ))
    centre = scale * np.cos(math.pi / (2 * NZ) * (order * (2 * height + 1) % (4 * NZ)))
    keep = (height < NZ - 1) & (order > 0)
    face = math.sqrt(2.0 / NZ) * np.sin(math.pi / NZ * (order * (height + 1) % (2 * NZ))) * keep
    return split(centre), split(face)


def home(row):
    if row < FRINGE:
        return row + ROWS - FRINGE
    if row >= ROWS - FRINGE:
        return row - (ROWS - FRINGE)
    return row


def plane_tables():
    half = NX // 2
    angle = 2.0 * math.pi / NX * (np.arange(half)[:, None] * np.arange(NX)[None, :] % NX)
    forward_x = np.concatenate([np.cos(angle), -np.sin(angle)], axis=0)
    weight = np.where(np.arange(half) == 0, 1.0, 2.0)[:, None] / NX
    inverse_x = np.concatenate([np.cos(angle) * weight, -np.sin(angle) * weight], axis=0).T
    order = np.concatenate([np.arange(CX) + CX * home(row) for row in range(ROWS)])
    inverse_x = inverse_x[order]
    angle = 2.0 * math.pi / NY * (np.arange(NY)[:, None] * np.arange(NY)[None, :] % NY)
    keep = (np.arange(NY) != NY // 2)[None, :]
    forward_y = np.concatenate([np.cos(angle) * keep, np.sin(angle) * keep], axis=1)
    inverse_y = np.concatenate([np.cos(angle), np.sin(angle)], axis=1) / NY
    return split(forward_x), split(forward_y), split(inverse_y), split(inverse_x)


def halves(x):
    high = x.astype(BF)
    low = (x - high.astype(F32)).astype(BF)
    return high, low


def thirds(x):
    high, rest = x.astype(BF), x
    rest = rest - high.astype(F32)
    middle = rest.astype(BF)
    rest = rest - middle.astype(F32)
    return rest.astype(BF), middle, high


def dot3(a, b, dims):
    one = functools.partial(lax.dot_general, dimension_numbers=(dims, ((), ())), preferred_element_type=F32)
    return one(a[0], b[0]) + (one(a[0], b[1]) + one(a[1], b[0]))


NN = ((1,), (0,))
NT = ((1,), (1,))
TN = ((0,), (0,))


def modes_kernel(field, centre, face, out):
    for c in range(3):
        table = face if c == 2 else centre
        x = field[c].reshape(CX * CY, NZ)
        out[pl.ds(c, NZ, stride=3), :] = dot3((table[0], table[1]), halves(x), NT)
    out[3 * NZ :, :] = jnp.zeros((3 * (ROWS * COLS - NZ), CX * CY), F32)


def swapped(x):
    row = lax.broadcasted_iota(jnp.int32, x.shape, 0)
    lane = lax.broadcasted_iota(jnp.int32, x.shape, 1)
    rows, lanes = x.shape
    for bit in range(4):
        by_row, by_lane = 1 << bit, 8 << bit
        row_bit = (row >> bit) & 1
        lane_bit = (lane >> (3 + bit)) & 1
        other = jnp.where(row_bit == 0, pltpu.roll(x, rows - by_row, 0), pltpu.roll(x, by_row, 0))
        moved = jnp.where(
            row_bit == 0, pltpu.roll(other, by_lane, 1), pltpu.roll(other, lanes - by_lane, 1)
        )
        x = jnp.where(row_bit == lane_bit, x, moved)
    return x


def plane_kernel(rise_ref, inp, fx, fy, iy, ix, out):
    half = NX // 2
    spec = []
    for c in range(3):
        x = swapped(inp[pl.ds(c, NX, stride=3), :])
        along = dot3((fx[0], fx[1]), halves(x), NN)
        both = dot3(halves(along), (fy[0], fy[1]), NN)
        re = both[:half, :NY] + both[half:, NY:]
        im = both[half:, :NY] - both[:half, NY:]
        spec.append((re, im))
    rise = rise_ref[0, 0]
    k = lax.broadcasted_iota(jnp.int32, (half, NY), 0)
    q = lax.broadcasted_iota(jnp.int32, (half, NY), 1)
    kx = (2.0 * math.pi / NX) * k.astype(F32)
    ky = (2.0 * math.pi / NY) * jnp.where(q < NY // 2, q, q - NY).astype(F32)
    hor = kx * kx + ky * ky
    bound = hor + rise * rise
    inverse = jnp.where(bound > 0.0, -1.0 / jnp.where(bound > 0.0, bound, 1.0), 0.0)
    decay = jnp.exp(-DIFFUSE * hor)
    (ur, ui), (vr, vi), (wr, wi) = spec
    press_re = (rise * wr - kx * ui - ky * vi) * inverse
    press_im = (rise * wi + kx * ur + ky * vr) * inverse
    new = (
        ((ur + kx * press_im) * decay, (ui - kx * press_re) * decay),
        ((vr + ky * press_im) * decay, (vi - ky * press_re) * decay),
        ((wr + rise * press_re) * decay, (wi + rise * press_im) * decay),
    )
    for c in range(3):
        both = dot3(halves(jnp.concatenate(new[c], axis=0)), (iy[0], iy[1]), NN)
        re = both[:half, :NY] - both[half:, NY:]
        im = both[:half, NY:] + both[half:, :NY]
        x = dot3((ix[0], ix[1]), halves(jnp.concatenate([re, im], axis=0)), NN)
        out[pl.ds(c, NX, stride=3), :] = swapped(x)


def levels_kernel(row_ref, modes, farm, centre, face, phys, state, low, high):
    fringe = row_ref[0] < FRINGE
    for c in range(3):
        table = face if c == 2 else centre
        x = modes[pl.ds(c, NZ, stride=3), :]
        y = dot3(halves(x), (table[0], table[1]), TN).reshape(CX, CY, NZ)
        phys[c] = y
        s = jnp.where(fringe, y, farm[c])
        state[c] = s
        low[c] = s[:2]
        high[c] = s[CX - 2 :]


def slot_force(u, index):
    column = index[0:1, :]
    level = index[1:2, :]
    turbine = index[2:3, :]
    at_column = jnp.where(
        lax.broadcasted_iota(jnp.int32, (CX * CY, SLOTS), 0) == column, 1.0, 0.0
    ).astype(BF)
    at_level = lax.broadcasted_iota(jnp.int32, (NZ, SLOTS), 0) == level
    owned = jnp.where(lax.broadcasted_iota(jnp.int32, (TURB, SLOTS), 0) == turbine, 1.0, 0.0)
    one = functools.partial(lax.dot_general, preferred_element_type=F32)
    picked = sum(one(part, at_column, dimension_numbers=(TN, ((), ()))) for part in thirds(u))
    values = jnp.sum(jnp.where(at_level, picked, 0.0), axis=0, keepdims=True) + WIND
    sums = jnp.sum(owned * values, axis=1, keepdims=True)
    counts = jnp.sum(owned, axis=1, keepdims=True)
    mean = sums / jnp.maximum(counts, 1.0)
    thrust = -0.5 * THRUST * mean * jnp.abs(mean)
    per_slot = jnp.sum(owned * thrust, axis=0, keepdims=True)
    parts = thirds(jnp.where(at_level, per_slot, 0.0))
    return sum(one(at_column, part, dimension_numbers=(NT, ((), ()))) for part in parts)


EXT = 16
OFF = 4


def stage_kernel(alpha, beta, cur, xlo, xhi, ylo, yhi, base, index, new, low, high, s, e, force):
    force[...] = slot_force(cur[0].reshape(CX * CY, NZ), index).reshape(CX, CY, NZ)
    s[...] = jnp.zeros(s.shape, F32)
    for c in range(3):
        s[c, 2 : CX + 2, OFF : OFF + CY, :NZ] = cur[c]
        s[c, 0:2, OFF : OFF + CY, :NZ] = xlo[c]
        s[c, CX + 2 :, OFF : OFF + CY, :NZ] = xhi[c]
        s[c, :, OFF - 2 : OFF, :NZ] = ylo[c]
        s[c, :, OFF + CY : OFF + CY + 2, :NZ] = yhi[c]

    def after_y(x):
        return pltpu.roll(x, EXT - 1, 0)

    def before_y(x):
        return pltpu.roll(x, 1, 0)

    def after_z(x):
        return pltpu.roll(x, LANES - 1, 1)

    def before_z(x):
        return pltpu.roll(x, 1, 1)

    diagonal = 0.5 * SMAG * SMAG
    cross = 0.25 * SMAG * SMAG

    def viscosity(p, carry):
        f = [s[c, p] for c in range(3)]
        dx = [s[c, p + 1] - s[c, p - 1] for c in range(3)]
        dy = [after_y(f[c]) - before_y(f[c]) for c in range(3)]
        dz = [after_z(f[c]) - before_z(f[c]) for c in range(3)]
        uv = dy[0] + dx[1]
        uw = dz[0] + dx[2]
        vw = dz[1] + dy[2]
        e[p] = jnp.sqrt(
            diagonal * (dx[0] * dx[0] + dy[1] * dy[1] + dz[2] * dz[2])
            + cross * (uv * uv + uw * uw + vw * vw)
        )
        return carry

    lax.fori_loop(1, CX + 3, viscosity, 0)

    def fluxes(speed, eddy, fa, fb):
        speed = 0.25 * speed
        eddy = 0.5 * eddy
        plus = speed + eddy
        minus = speed - eddy
        return [plus * fa[c] + minus * fb[c] for c in range(3)]

    def face(p):
        fa = [s[c, p] for c in range(3)]
        fb = [s[c, p + 1] for c in range(3)]
        return fluxes(fa[0] + fb[0] + 2.0 * WIND, e[p] + e[p + 1], fa, fb)

    def advance(p, below):
        f = [s[c, p] for c in range(3)]
        eddy = e[p]
        above = face(p)
        fy = [after_y(f[c]) for c in range(3)]
        along_y = fluxes(f[1] + fy[1], eddy + after_y(eddy), f, fy)
        fz = [after_z(f[c]) for c in range(3)]
        along_z = fluxes(f[2] + fz[2], eddy + after_z(eddy), f, fz)
        for c in range(3):
            rate = (
                below[c]
                - above[c]
                + (before_y(along_y[c]) - along_y[c])
                + (before_z(along_z[c]) - along_z[c])
            )
            rate = rate[OFF : OFF + CY, :NZ]
            if c == 0:
                rate = rate + force[p - 2]
            value = beta * (cur[c, p - 2] + STEP * rate)
            if alpha != 0.0:
                value = value + alpha * base[c, p - 2]
            new[c, p - 2] = value
        return above

    lax.fori_loop(2, CX + 2, advance, face(1))
    for c in range(3):
        low[c] = new[c, :2]
        high[c] = new[c, CX - 2 :]


def sds(*shape):
    return jax.ShapeDtypeStruct(shape, F32)


VM = pl.BlockSpec(memory_space=pltpu.VMEM)
SM = pl.BlockSpec(memory_space=pltpu.SMEM)
LIMIT = pltpu.CompilerParams(vmem_limit_bytes=48 << 20)


def exchange(value):
    whole = value.reshape(ROWS * COLS, 1, 3 * CX * CY)
    whole = lax.all_to_all(whole, ("gx", "gy"), 0, 0, tiled=True)
    return whole.reshape(3 * ROWS * COLS, CX * CY)


def ring(value, axis, steps):
    count = lax.axis_size(axis)
    return lax.ppermute(value, axis, [(i, (i + steps) % count) for i in range(count)])


def shards(farm_velocity, precursor_velocity, turb_cell, turb_slot, disk_mask):
    row = lax.axis_index("gx")
    column = lax.axis_index("gy")
    centre, face = (jnp.asarray(t) for t in vertical_tables())
    tables = [jnp.asarray(t) for t in plane_tables()]
    order = (row * COLS + column).astype(F32)
    rise = (2.0 * jnp.sin(order * (math.pi / (2 * NZ)))).reshape(1, 1)
    with jax.named_scope("vertical_modes"):
        modes = pl.pallas_call(
            modes_kernel,
            out_shape=sds(3 * ROWS * COLS, CX * CY),
            in_specs=[VM] * 3,
            out_specs=VM,
            compiler_params=LIMIT,
        )(precursor_velocity, centre, face)
        modes = exchange(modes)
    with jax.named_scope("planes"):
        modes = pl.pallas_call(
            plane_kernel,
            out_shape=sds(3 * ROWS * COLS, CX * CY),
            in_specs=[SM] + [VM] * 5,
            out_specs=VM,
            compiler_params=LIMIT,
        )(rise, modes, *tables)
        modes = exchange(modes)
    with jax.named_scope("levels"):
        phys, state, low, high = pl.pallas_call(
            levels_kernel,
            out_shape=(sds(3, CX, CY, NZ), sds(3, CX, CY, NZ), sds(3, 2, CY, NZ), sds(3, 2, CY, NZ)),
            in_specs=[SM] + [VM] * 4,
            out_specs=(VM,) * 4,
            compiler_params=LIMIT,
        )(row.reshape(1).astype(jnp.int32), modes, farm_velocity, centre, face)
    cell = turb_cell.reshape(1, SLOTS)
    slot = jnp.where(disk_mask.reshape(1, SLOTS) == 1, turb_slot.reshape(1, SLOTS), -1)
    index = jnp.concatenate([cell // NZ, cell % NZ, slot, jnp.zeros((5, SLOTS), jnp.int32)], axis=0)

    precursor_new = lax.ppermute(phys, "gx", [(home(i), i) for i in range(ROWS)])

    current = state
    for alpha, beta in ((0.0, 1.0), (0.75, 0.25), (1.0 / 3.0, 2.0 / 3.0)):
        with jax.named_scope("halo"):
            xlo = ring(high, "gx", 1)
            xhi = ring(low, "gx", -1)
            first = jnp.concatenate([xlo[:, :, :2], current[:, :, :2], xhi[:, :, :2]], axis=1)
            last = jnp.concatenate(
                [xlo[:, :, CY - 2 :], current[:, :, CY - 2 :], xhi[:, :, CY - 2 :]], axis=1
            )
            ylo = ring(last, "gy", 1)
            yhi = ring(first, "gy", -1)
        with jax.named_scope("section"):
            current, low, high = pl.pallas_call(
                functools.partial(stage_kernel, alpha, beta),
                out_shape=(sds(3, CX, CY, NZ), sds(3, 2, CY, NZ), sds(3, 2, CY, NZ)),
                in_specs=[VM] * 7,
                out_specs=(VM,) * 3,
                scratch_shapes=[
                    pltpu.VMEM((3, CX + 4, EXT, LANES), F32),
                    pltpu.VMEM((CX + 4, EXT, LANES), F32),
                    pltpu.VMEM((CX, CY, NZ), F32),
                ],
                compiler_params=LIMIT,
            )(current, xlo, xhi, ylo, yhi, state, index)
    return current, precursor_new


def solution(mesh):
    return jax.shard_map(
        shards,
        mesh=mesh,
        in_specs=(
            P(None, "gx", "gy", None),
            P(None, "gx", "gy", None),
            P("gx", "gy", None),
            P("gx", "gy", None),
            P("gx", "gy", None),
        ),
        out_specs=(P(None, "gx", "gy", None), P(None, "gx", "gy", None)),
        check_vma=False,
    )
```

```python
import functools
import math

import jax
import jax.numpy as jnp
import ml_dtypes
import numpy as np
from jax import lax
from jax.experimental import pallas as pl
from jax.experimental.pallas import tpu as pltpu
from jax.sharding import PartitionSpec as P

NF = 48
TURB = 16
WIND = 3.0
STEP = 0.1
SMAG = 0.0289
THRUST = 1.33
DIFFUSE = 0.05

CX, CY, NZ = 16, 8, 192
NX, NY = 256, 128
ROWS, COLS = 16, 16
SLOTS = 256
FRINGE = NF // CX
LANES = 256

BF = jnp.bfloat16
F32 = jnp.float32


def split(table):
    table = np.asarray(table, np.float64)
    high = table.astype(np.float32).astype(ml_dtypes.bfloat16)
    low = (table - high.astype(np.float64)).astype(np.float32).astype(ml_dtypes.bfloat16)
    return np.stack([high, low])


def vertical_tables():
    height = np.arange(NZ)[None, :]
    order = np.arange(NZ)[:, None]
    scale = np.where(order == 0, math.sqrt(1.0 / NZ), math.sqrt(2.0 / NZ))
    centre = scale * np.cos(math.pi / (2 * NZ) * (order * (2 * height + 1) % (4 * NZ)))
    keep = (height < NZ - 1) & (order > 0)
    face = math.sqrt(2.0 / NZ) * np.sin(math.pi / NZ * (order * (height + 1) % (2 * NZ))) * keep
    return split(centre), split(face)


def home(row):
    if row < FRINGE:
        return row + ROWS - FRINGE
    if row >= ROWS - FRINGE:
        return row - (ROWS - FRINGE)
    return row


def plane_tables():
    half = NX // 2
    angle = 2.0 * math.pi / NX * (np.arange(half)[:, None] * np.arange(NX)[None, :] % NX)
    forward_x = np.concatenate([np.cos(angle), -np.sin(angle)], axis=0)
    weight = np.where(np.arange(half) == 0, 1.0, 2.0)[:, None] / NX
    inverse_x = np.concatenate([np.cos(angle) * weight, -np.sin(angle) * weight], axis=0).T
    order = np.concatenate([np.arange(CX) + CX * home(row) for row in range(ROWS)])
    inverse_x = inverse_x[order]
    angle = 2.0 * math.pi / NY * (np.arange(NY)[:, None] * np.arange(NY)[None, :] % NY)
    keep = (np.arange(NY) != NY // 2)[None, :]
    forward_y = np.concatenate([np.cos(angle) * keep, np.sin(angle) * keep], axis=1)
    inverse_y = np.concatenate([np.cos(angle), np.sin(angle)], axis=1) / NY
    return split(forward_x), split(forward_y), split(inverse_y), split(inverse_x)


def halves(x):
    high = x.astype(BF)
    low = (x - high.astype(F32)).astype(BF)
    return high, low


def thirds(x):
    high, rest = x.astype(BF), x
    rest = rest - high.astype(F32)
    middle = rest.astype(BF)
    rest = rest - middle.astype(F32)
    return rest.astype(BF), middle, high


def dot3(a, b, dims):
    one = functools.partial(lax.dot_general, dimension_numbers=(dims, ((), ())), preferred_element_type=F32)
    return one(a[0], b[0]) + (one(a[0], b[1]) + one(a[1], b[0]))


NN = ((1,), (0,))
NT = ((1,), (1,))
TN = ((0,), (0,))


def modes_kernel(field_hbm, centre_hbm, face_hbm, out, field, centre, face, done):
    copies = [
        pltpu.make_async_copy(centre_hbm, centre, done.at[0]),
        pltpu.make_async_copy(field_hbm.at[0], field.at[0], done.at[1]),
        pltpu.make_async_copy(field_hbm.at[1], field.at[1], done.at[2]),
        pltpu.make_async_copy(face_hbm, face, done.at[3]),
        pltpu.make_async_copy(field_hbm.at[2], field.at[2], done.at[4]),
    ]
    for copy in copies:
        copy.start()
    out[3 * NZ :, :] = jnp.zeros((3 * (ROWS * COLS - NZ), CX * CY), F32)
    for c, ready in ((0, copies[:2]), (1, copies[2:3]), (2, copies[3:])):
        for copy in ready:
            copy.wait()
        table = face if c == 2 else centre
        x = field[c].reshape(CX * CY, NZ)
        out[pl.ds(c, NZ, stride=3), :] = dot3((table[0], table[1]), halves(x), NT)


def swap_masks():
    row = lax.broadcasted_iota(jnp.int32, (8, CX * CY), 0)
    lane = lax.broadcasted_iota(jnp.int32, (8, CX * CY), 1)
    masks = []
    for bit in range(3):
        row_bit = (row >> bit) & 1
        lane_bit = (lane >> (3 + bit)) & 1
        masks.append(((row_bit < lane_bit), (row_bit > lane_bit), row_bit == 0))
    return masks, lane >= 64


def swapped(parts, masks):
    masks, upper = masks
    low, high = parts
    low, high = (
        jnp.where(upper, pltpu.roll(high, 64, 1), low),
        jnp.where(upper, high, pltpu.roll(low, 64, 1)),
    )
    out = []
    for x in (low, high):
        for bit in range(3):
            later, earlier, even = masks[bit]
            by_row, by_lane = 1 << bit, 8 << bit
            other = pltpu.roll(x, by_row, 0)
            if by_row != 4:
                other = jnp.where(even, pltpu.roll(x, 8 - by_row, 0), other)
            x = jnp.where(
                later,
                pltpu.roll(other, by_lane, 1),
                jnp.where(earlier, pltpu.roll(other, CX * CY - by_lane, 1), x),
            )
        out.append(x)
    return out


def plane_kernel(rise_ref, inp, fx, fy, iy, ix, out):
    half = NX // 2
    masks = swap_masks()
    spec = []
    for c in range(3):
        rows = []
        for r in range(2 * ROWS):
            rows.append(inp[pl.ds(24 * r + c, 8, stride=3), :])
            if r % 2 == 1:
                rows[-2:] = swapped(rows[-2:], masks)
        x = jnp.concatenate(rows, axis=0)
        along = dot3((fx[0], fx[1]), halves(x), NN)
        both = dot3(halves(along), (fy[0], fy[1]), NN)
        re = both[:half, :NY] + both[half:, NY:]
        im = both[half:, :NY] - both[:half, NY:]
        spec.append((re, im))
    rise = rise_ref[0, 0]
    k = lax.broadcasted_iota(jnp.int32, (half, NY), 0)
    q = lax.broadcasted_iota(jnp.int32, (half, NY), 1)
    kx = (2.0 * math.pi / NX) * k.astype(F32)
    ky = (2.0 * math.pi / NY) * jnp.where(q < NY // 2, q, q - NY).astype(F32)
    hor = kx * kx + ky * ky
    bound = hor + rise * rise
    inverse = jnp.where(bound > 0.0, -1.0 / jnp.where(bound > 0.0, bound, 1.0), 0.0)
    decay = jnp.exp(-DIFFUSE * hor)
    (ur, ui), (vr, vi), (wr, wi) = spec
    press_re = (rise * wr - kx * ui - ky * vi) * inverse
    press_im = (rise * wi + kx * ur + ky * vr) * inverse
    new = (
        ((ur + kx * press_im) * decay, (ui - kx * press_re) * decay),
        ((vr + ky * press_im) * decay, (vi - ky * press_re) * decay),
        ((wr + rise * press_re) * decay, (wi + rise * press_im) * decay),
    )
    for c in range(3):
        both = dot3(halves(jnp.concatenate(new[c], axis=0)), (iy[0], iy[1]), NN)
        re = both[:half, :NY] - both[half:, NY:]
        im = both[:half, NY:] + both[half:, :NY]
        x = dot3((ix[0], ix[1]), halves(jnp.concatenate([re, im], axis=0)), NN)
        for r in range(ROWS):
            pair = swapped((x[16 * r : 16 * r + 8], x[16 * r + 8 : 16 * r + 16]), masks)
            for side in range(2):
                out[pl.ds(48 * r + 24 * side + c, 8, stride=3), :] = pair[side]


def levels_kernel(row_ref, modes, farm, centre, face, phys, state, low, high):
    fringe = row_ref[0] < FRINGE
    for c in range(3):
        table = face if c == 2 else centre
        x = modes[pl.ds(c, NZ, stride=3), :]
        y = dot3(halves(x), (table[0], table[1]), TN).reshape(CX, CY, NZ)
        phys[c] = y
        s = jnp.where(fringe, y, farm[c])
        state[c] = s
        low[c] = s[:2]
        high[c] = s[CX - 2 :]


def slot_force(u, index):
    column = index[0:1, :]
    level = index[1:2, :]
    turbine = index[2:3, :]
    at_column = jnp.where(
        lax.broadcasted_iota(jnp.int32, (CX * CY, SLOTS), 0) == column, 1.0, 0.0
    ).astype(BF)
    at_level = lax.broadcasted_iota(jnp.int32, (NZ, SLOTS), 0) == level
    owned = jnp.where(lax.broadcasted_iota(jnp.int32, (TURB, SLOTS), 0) == turbine, 1.0, 0.0)
    one = functools.partial(lax.dot_general, preferred_element_type=F32)
    picked = sum(one(part, at_column, dimension_numbers=(TN, ((), ()))) for part in thirds(u))
    values = jnp.sum(jnp.where(at_level, picked, 0.0), axis=0, keepdims=True) + WIND
    sums = jnp.sum(owned * values, axis=1, keepdims=True)
    counts = jnp.sum(owned, axis=1, keepdims=True)
    mean = sums / jnp.maximum(counts, 1.0)
    thrust = -0.5 * THRUST * mean * jnp.abs(mean)
    per_slot = jnp.sum(owned * thrust, axis=0, keepdims=True)
    parts = thirds(jnp.where(at_level, per_slot, 0.0))
    return sum(one(at_column, part, dimension_numbers=(NT, ((), ()))) for part in parts)


EXT = 16
OFF = 4
DIAGONAL = 0.5 * SMAG * SMAG
CROSS = 0.25 * SMAG * SMAG


def force_kernel(cur, index, force):
    force[...] = slot_force(cur[...].reshape(CX * CY, NZ), index).reshape(CX, CY, NZ)


def after_y(x):
    return pltpu.roll(x, EXT - 1, 0)


def before_y(x):
    return pltpu.roll(x, 1, 0)


def after_z(x):
    return pltpu.roll(x, LANES - 1, 1)


def before_z(x):
    return pltpu.roll(x, 1, 1)


def assemble(s, cur, xlo, xhi, ylo, yhi, begin, end):
    for c in range(3):
        s[c, begin:end] = jnp.zeros((end - begin, EXT, LANES), F32)
        own = slice(max(begin, 2), min(end, CX + 2))
        s[c, own, OFF : OFF + CY, :NZ] = cur[c, own.start - 2 : own.stop - 2]
        if begin < 2:
            s[c, begin:2, OFF : OFF + CY, :NZ] = xlo[c, begin:2]
        if end > CX + 2:
            s[c, CX + 2 : end, OFF : OFF + CY, :NZ] = xhi[c, : end - CX - 2]
        near = slice(max(begin, 1), min(end, CX + 3))
        s[c, near, OFF - 2 : OFF, :NZ] = ylo[c, near.start - 1 : near.stop - 1]
        s[c, near, OFF + CY : OFF + CY + 2, :NZ] = yhi[c, near.start - 1 : near.stop - 1]


def viscosity(s, e, p):
    f = [s[c, p] for c in range(3)]
    dx = [s[c, p + 1] - s[c, p - 1] for c in range(3)]
    dy = [after_y(f[c]) - before_y(f[c]) for c in range(3)]
    dz = [after_z(f[c]) - before_z(f[c]) for c in range(3)]
    uv = dy[0] + dx[1]
    uw = dz[0] + dx[2]
    vw = dz[1] + dy[2]
    e[p] = jnp.sqrt(
        DIAGONAL * (dx[0] * dx[0] + dy[1] * dy[1] + dz[2] * dz[2])
        + CROSS * (uv * uv + uw * uw + vw * vw)
    )


def fluxes(speed, eddy, fa, fb):
    speed = 0.25 * speed
    eddy = 0.5 * eddy
    plus = speed + eddy
    minus = speed - eddy
    return [plus * fa[c] + minus * fb[c] for c in range(3)]


def face(s, e, p):
    fa = [s[c, p] for c in range(3)]
    fb = [s[c, p + 1] for c in range(3)]
    return fluxes(fa[0] + fb[0] + 2.0 * WIND, e[p] + e[p + 1], fa, fb)


def advance(alpha, beta, s, e, force, base, store, p, below):
    f = [s[c, p] for c in range(3)]
    eddy = e[p]
    above = face(s, e, p)
    fy = [after_y(f[c]) for c in range(3)]
    along_y = fluxes(f[1] + fy[1], eddy + after_y(eddy), f, fy)
    fz = [after_z(f[c]) for c in range(3)]
    along_z = fluxes(f[2] + fz[2], eddy + after_z(eddy), f, fz)
    for c in range(3):
        rate = (
            below[c]
            - above[c]
            + (before_y(along_y[c]) - along_y[c])
            + (before_z(along_z[c]) - along_z[c])
        )
        value = (beta * (f[c] + STEP * rate))[OFF : OFF + CY, :NZ]
        if c == 0:
            value = value + (beta * STEP) * force[p - 2]
        if alpha != 0.0:
            value = value + alpha * base[c, p - 2]
        store(c, p - 2, value)
    return above


def edge_kernel(alpha, beta, cur, xlo, xhi, ylo, yhi, base, force, low, high, s, e):
    assemble(s, cur, xlo, xhi, ylo, yhi, 0, 6)
    assemble(s, cur, xlo, xhi, ylo, yhi, CX - 2, CX + 4)
    for start, out in ((2, low), (CX, high)):
        for p in range(start - 1, start + 3):
            viscosity(s, e, p)

        def store(c, x, value, out=out, start=start):
            out[c, x + 2 - start] = value

        below = face(s, e, start - 1)
        for p in (start, start + 1):
            below = advance(alpha, beta, s, e, force, base, store, p, below)


def whole_kernel(alpha, beta, cur, xlo, xhi, ylo, yhi, base, force, other, new, kept, s, e, done):
    copy = pltpu.make_async_copy(other, kept, done)
    copy.start()
    assemble(s, cur, xlo, xhi, ylo, yhi, 0, CX + 4)

    for p in range(1, CX + 3):
        viscosity(s, e, p)

    def store(c, x, value):
        new[c, x] = value

    below = face(s, e, 1)
    for p in range(2, CX + 2):
        below = advance(alpha, beta, s, e, force, base, store, p, below)
    copy.wait()


def inner_kernel(alpha, beta, cur, xlo, xhi, ylo, yhi, base, force, low, high, new, s, e):
    assemble(s, cur, xlo, xhi, ylo, yhi, 2, CX + 2)

    for p in range(3, CX + 1):
        viscosity(s, e, p)

    def store(c, x, value):
        new[c, x] = value

    below = face(s, e, 3)
    for p in range(4, CX):
        below = advance(alpha, beta, s, e, force, base, store, p, below)
    for c in range(3):
        new[c, :2] = low[c]
        new[c, CX - 2 :] = high[c]


def sds(*shape):
    return jax.ShapeDtypeStruct(shape, F32)


def cost(micros):
    return pl.CostEstimate(flops=1000000 * micros, bytes_accessed=3000000 * micros, transcendentals=0)


VM = pl.BlockSpec(memory_space=pltpu.VMEM)
SM = pl.BlockSpec(memory_space=pltpu.SMEM)
LIMIT = pltpu.CompilerParams(vmem_limit_bytes=48 << 20)


def exchange(value):
    whole = value.reshape(ROWS * COLS, 1, 3 * CX * CY)
    whole = lax.all_to_all(whole, ("gx", "gy"), 0, 0, tiled=True)
    return whole.reshape(3 * ROWS * COLS, CX * CY)


def ring(value, axis, steps):
    count = lax.axis_size(axis)
    return lax.ppermute(value, axis, [(i, (i + steps) % count) for i in range(count)])


def shards(farm_velocity, precursor_velocity, turb_cell, turb_slot, disk_mask):
    row = lax.axis_index("gx")
    column = lax.axis_index("gy")
    centre, face = (jnp.asarray(t) for t in vertical_tables())
    tables = [jnp.asarray(t) for t in plane_tables()]
    order = (row * COLS + column).astype(F32)
    rise = (2.0 * jnp.sin(order * (math.pi / (2 * NZ)))).reshape(1, 1)
    with jax.named_scope("vertical_modes"):
        modes = pl.pallas_call(
            modes_kernel,
            out_shape=sds(3 * ROWS * COLS, CX * CY),
            in_specs=[pl.BlockSpec(memory_space=pltpu.HBM)] * 3,
            out_specs=VM,
            scratch_shapes=[
                pltpu.VMEM((3, CX, CY, NZ), F32),
                pltpu.VMEM((2, NZ, NZ), BF),
                pltpu.VMEM((2, NZ, NZ), BF),
                pltpu.SemaphoreType.DMA((5,)),
            ],
            compiler_params=pltpu.CompilerParams(vmem_limit_bytes=60 << 20),
        )(precursor_velocity, centre, face)
        modes = exchange(modes)
    with jax.named_scope("planes"):
        modes = pl.pallas_call(
            plane_kernel,
            out_shape=sds(3 * ROWS * COLS, CX * CY),
            in_specs=[SM] + [VM] * 5,
            out_specs=VM,
            compiler_params=LIMIT,
        )(rise, modes, *tables)
        modes = exchange(modes)
    with jax.named_scope("levels"):
        phys, state, low, high = pl.pallas_call(
            levels_kernel,
            out_shape=(sds(3, CX, CY, NZ), sds(3, CX, CY, NZ), sds(3, 2, CY, NZ), sds(3, 2, CY, NZ)),
            in_specs=[SM] + [VM] * 4,
            out_specs=(VM,) * 4,
            compiler_params=LIMIT,
        )(row.reshape(1).astype(jnp.int32), modes, farm_velocity, centre, face)
    cell = turb_cell.reshape(1, SLOTS)
    slot = jnp.where(disk_mask.reshape(1, SLOTS) == 1, turb_slot.reshape(1, SLOTS), -1)
    index = jnp.concatenate([cell // NZ, cell % NZ, slot, jnp.zeros((5, SLOTS), jnp.int32)], axis=0)

    precursor_new = lax.ppermute(phys, "gx", [(home(i), i) for i in range(ROWS)])

    current = state
    weights = ((0.0, 1.0), (0.75, 0.25), (1.0 / 3.0, 2.0 / 3.0))
    for section, (alpha, beta) in enumerate(weights):
        with jax.named_scope("drag"):
            force = pl.pallas_call(
                force_kernel,
                grid=(1,),
                out_shape=sds(CX, CY, NZ),
                in_specs=[
                    pl.BlockSpec((None, CX, CY, NZ), lambda i: (0, 0, 0, 0)),
                    pl.BlockSpec((8, SLOTS), lambda i: (0, 0)),
                ],
                out_specs=pl.BlockSpec((CX, CY, NZ), lambda i: (0, 0, 0)),
                compiler_params=LIMIT,
                cost_estimate=cost(1),
            )(current, index)
        with jax.named_scope("halo"):
            xlo = ring(high, "gx", 1)
            xhi = ring(low, "gx", -1)
            first = jnp.concatenate([xlo[:, 1:, :2], current[:, :, :2], xhi[:, :1, :2]], axis=1)
            last = jnp.concatenate(
                [xlo[:, 1:, CY - 2 :], current[:, :, CY - 2 :], xhi[:, :1, CY - 2 :]], axis=1
            )
            ylo = ring(last, "gy", 1)
            yhi = ring(first, "gy", -1)
        scratch = [
            pltpu.VMEM((3, CX + 4, EXT, LANES), F32),
            pltpu.VMEM((CX + 4, EXT, LANES), F32),
        ]
        operands = (current, xlo, xhi, ylo, yhi, state, force)
        if section == 2:
            with jax.named_scope("whole"):
                current, precursor_new = pl.pallas_call(
                    functools.partial(whole_kernel, alpha, beta),
                    out_shape=(sds(3, CX, CY, NZ),) * 2,
                    in_specs=[VM] * 7 + [pl.BlockSpec(memory_space=pl.ANY)],
                    out_specs=(VM, pl.BlockSpec(memory_space=pl.ANY)),
                    scratch_shapes=scratch + [pltpu.SemaphoreType.DMA],
                    compiler_params=LIMIT,
                    cost_estimate=cost(5),
                )(*operands, precursor_new)
            break
        with jax.named_scope("edge"):
            low, high = pl.pallas_call(
                functools.partial(edge_kernel, alpha, beta),
                out_shape=(sds(3, 2, CY, NZ),) * 2,
                in_specs=[VM] * 7,
                out_specs=(VM,) * 2,
                scratch_shapes=scratch,
                compiler_params=LIMIT,
                cost_estimate=cost(2),
            )(*operands)
        with jax.named_scope("inner"):
            current = pl.pallas_call(
                functools.partial(inner_kernel, alpha, beta),
                out_shape=sds(3, CX, CY, NZ),
                in_specs=[VM] * 9,
                out_specs=VM,
                scratch_shapes=scratch,
                compiler_params=LIMIT,
                cost_estimate=cost(4),
            )(*operands, low, high)
    return current, precursor_new


def solution(mesh):
    return jax.shard_map(
        shards,
        mesh=mesh,
        in_specs=(
            P(None, "gx", "gy", None),
            P(None, "gx", "gy", None),
            P("gx", "gy", None),
            P("gx", "gy", None),
            P("gx", "gy", None),
        ),
        out_specs=(P(None, "gx", "gy", None), P(None, "gx", "gy", None)),
        check_vma=False,
    )
```

```python
import functools
import math

import jax
import jax.numpy as jnp
import ml_dtypes
import numpy as np
from jax import lax
from jax.experimental import pallas as pl
from jax.experimental.pallas import tpu as pltpu
from jax.sharding import PartitionSpec as P

NF = 48
TURB = 16
WIND = 3.0
STEP = 0.1
SMAG = 0.0289
THRUST = 1.33
DIFFUSE = 0.05

CX, CY, NZ = 16, 8, 192
NX, NY = 256, 128
ROWS, COLS = 16, 16
SLOTS = 256
FRINGE = NF // CX
LANES = 256

BF = jnp.bfloat16
F32 = jnp.float32


def split(table):
    table = np.asarray(table, np.float64)
    high = table.astype(np.float32).astype(ml_dtypes.bfloat16)
    low = (table - high.astype(np.float64)).astype(np.float32).astype(ml_dtypes.bfloat16)
    return np.stack([high, low])


def vertical_tables():
    height = np.arange(NZ)[None, :]
    order = np.arange(NZ)[:, None]
    scale = np.where(order == 0, math.sqrt(1.0 / NZ), math.sqrt(2.0 / NZ))
    centre = scale * np.cos(math.pi / (2 * NZ) * (order * (2 * height + 1) % (4 * NZ)))
    keep = (height < NZ - 1) & (order > 0)
    face = math.sqrt(2.0 / NZ) * np.sin(math.pi / NZ * (order * (height + 1) % (2 * NZ))) * keep
    return split(centre), split(face)


def home(row):
    if row < FRINGE:
        return row + ROWS - FRINGE
    if row >= ROWS - FRINGE:
        return row - (ROWS - FRINGE)
    return row


def plane_tables():
    half = NX // 2
    angle = 2.0 * math.pi / NX * (np.arange(half)[:, None] * np.arange(NX)[None, :] % NX)
    forward_x = np.concatenate([np.cos(angle), -np.sin(angle)], axis=0)
    weight = np.where(np.arange(half) == 0, 1.0, 2.0)[:, None] / NX
    inverse_x = np.concatenate([np.cos(angle) * weight, -np.sin(angle) * weight], axis=0).T
    order = np.concatenate([np.arange(CX) + CX * home(row) for row in range(ROWS)])
    places = (CX * np.arange(ROWS)[:, None] + np.array([-2, -1, CX, CX + 1])[None, :]) % NX
    source = np.where(places < NF, NX - NF + places, 0)
    beside = inverse_x[np.repeat(source.reshape(-1), 4)]
    inverse_x = inverse_x[order]
    angle = 2.0 * math.pi / NY * (np.arange(NY)[:, None] * np.arange(NY)[None, :] % NY)
    keep = (np.arange(NY) != NY // 2)[None, :]
    forward_y = np.concatenate([np.cos(angle) * keep, np.sin(angle) * keep], axis=1)
    inverse_y = np.concatenate([np.cos(angle), np.sin(angle)], axis=1) / NY
    return split(forward_x), split(forward_y), split(inverse_y), split(inverse_x), split(beside)


def halves(x):
    high = x.astype(BF)
    low = (x - high.astype(F32)).astype(BF)
    return high, low


def thirds(x):
    high, rest = x.astype(BF), x
    rest = rest - high.astype(F32)
    middle = rest.astype(BF)
    rest = rest - middle.astype(F32)
    return rest.astype(BF), middle, high


def dot3(a, b, dims):
    one = functools.partial(lax.dot_general, dimension_numbers=(dims, ((), ())), preferred_element_type=F32)
    return one(a[0], b[0]) + (one(a[0], b[1]) + one(a[1], b[0]))


NN = ((1,), (0,))
NT = ((1,), (1,))
TN = ((0,), (0,))


def modes_kernel(field_hbm, centre_hbm, face_hbm, out, field, centre, face, done):
    copies = [
        pltpu.make_async_copy(centre_hbm, centre, done.at[0]),
        pltpu.make_async_copy(field_hbm.at[0], field.at[0], done.at[1]),
        pltpu.make_async_copy(field_hbm.at[1], field.at[1], done.at[2]),
        pltpu.make_async_copy(face_hbm, face, done.at[3]),
        pltpu.make_async_copy(field_hbm.at[2], field.at[2], done.at[4]),
    ]
    for copy in copies:
        copy.start()
    out[3 * NZ :, :] = jnp.zeros((3 * (ROWS * COLS - NZ), CX * CY), F32)
    for c, ready in ((0, copies[:2]), (1, copies[2:3]), (2, copies[3:])):
        for copy in ready:
            copy.wait()
        table = face if c == 2 else centre
        x = field[c].reshape(CX * CY, NZ)
        out[pl.ds(c, NZ, stride=3), :] = dot3((table[0], table[1]), halves(x), NT)


def swap_masks():
    row = lax.broadcasted_iota(jnp.int32, (8, CX * CY), 0)
    lane = lax.broadcasted_iota(jnp.int32, (8, CX * CY), 1)
    masks = []
    for bit in range(3):
        row_bit = (row >> bit) & 1
        lane_bit = (lane >> (3 + bit)) & 1
        masks.append(((row_bit < lane_bit), (row_bit > lane_bit), row_bit == 0))
    return masks, lane >= 64


def swapped(parts, masks):
    masks, upper = masks
    low, high = parts
    low, high = (
        jnp.where(upper, pltpu.roll(high, 64, 1), low),
        jnp.where(upper, high, pltpu.roll(low, 64, 1)),
    )
    out = []
    for x in (low, high):
        for bit in range(3):
            later, earlier, even = masks[bit]
            by_row, by_lane = 1 << bit, 8 << bit
            other = pltpu.roll(x, by_row, 0)
            if by_row != 4:
                other = jnp.where(even, pltpu.roll(x, 8 - by_row, 0), other)
            x = jnp.where(
                later,
                pltpu.roll(other, by_lane, 1),
                jnp.where(earlier, pltpu.roll(other, CX * CY - by_lane, 1), x),
            )
        out.append(x)
    return out


CHUNK = 6


def halo_slots(own, near):
    part = lax.broadcasted_iota(jnp.int32, own.shape, 0) % 4
    slot = lax.broadcasted_iota(jnp.int32, own.shape, 1) % 8
    across = jnp.where(slot < 2, pltpu.roll(own, 2, 1), pltpu.roll(own, 122, 1))
    corner = jnp.where(slot < 6, pltpu.roll(near, 6, 1), pltpu.roll(near, 126, 1))
    along = jnp.where(part == 0, pltpu.roll(near, 4, 1), jnp.where(part == 1, near, corner))
    return jnp.where(slot < 4, across, along)


def plane_kernel(rise_ref, inp, fx, fy, iy, ix, ix2, out):
    half = NX // 2
    masks = swap_masks()
    spec = []
    for c in range(3):
        rows = []
        for r in range(2 * ROWS):
            rows.append(inp[pl.ds(24 * r + c, 8, stride=3), :])
            if r % 2 == 1:
                rows[-2:] = swapped(rows[-2:], masks)
        x = jnp.concatenate(rows, axis=0)
        along = dot3((fx[0], fx[1]), halves(x), NN)
        both = dot3(halves(along), (fy[0], fy[1]), NN)
        re = both[:half, :NY] + both[half:, NY:]
        im = both[half:, :NY] - both[:half, NY:]
        spec.append((re, im))
    rise = rise_ref[0, 0]
    k = lax.broadcasted_iota(jnp.int32, (half, NY), 0)
    q = lax.broadcasted_iota(jnp.int32, (half, NY), 1)
    kx = (2.0 * math.pi / NX) * k.astype(F32)
    ky = (2.0 * math.pi / NY) * jnp.where(q < NY // 2, q, q - NY).astype(F32)
    hor = kx * kx + ky * ky
    bound = hor + rise * rise
    inverse = jnp.where(bound > 0.0, -1.0 / jnp.where(bound > 0.0, bound, 1.0), 0.0)
    decay = jnp.exp(-DIFFUSE * hor)
    (ur, ui), (vr, vi), (wr, wi) = spec
    press_re = (rise * wr - kx * ui - ky * vi) * inverse
    press_im = (rise * wi + kx * ur + ky * vr) * inverse
    new = (
        ((ur + kx * press_im) * decay, (ui - kx * press_re) * decay),
        ((vr + ky * press_im) * decay, (vi - ky * press_re) * decay),
        ((wr + rise * press_re) * decay, (wi + rise * press_im) * decay),
    )
    for c in range(3):
        both = dot3(halves(jnp.concatenate(new[c], axis=0)), (iy[0], iy[1]), NN)
        re = both[:half, :NY] - both[half:, NY:]
        im = both[:half, NY:] + both[half:, :NY]
        lines = halves(jnp.concatenate([re, im], axis=0))
        x = dot3((ix[0], ix[1]), lines, NN)
        near = dot3((ix2[0], ix2[1]), lines, NN)
        for r in range(ROWS):
            here = [slice(16 * r + 8 * side, 16 * r + 8 * side + 8) for side in range(2)]
            own = [x[rows] for rows in here]
            pair = swapped(own, masks)
            halo = swapped([halo_slots(own[side], near[here[side]]) for side in range(2)], masks)
            for side in range(2):
                first = CHUNK * (16 * r + 8 * side)
                out[pl.ds(first + c, 8, stride=CHUNK), :] = pair[side]
                out[pl.ds(first + 3 + c, 8, stride=CHUNK), :] = halo[side]


def levels_kernel(
    row_ref, modes, farm, fxlo, fxhi, fylo, fyhi, centre, face, phys, state, xlo, xhi, ylo, yhi, q
):
    row = row_ref[0]
    fringe = row < FRINGE
    below = (row >= 1) & (row <= FRINGE)
    above = (row < FRINGE - 1) | (row == ROWS - 1)
    for c in range(3):
        table = face if c == 2 else centre
        x = modes[pl.ds(c, NZ, stride=CHUNK), :]
        y = dot3(halves(x), (table[0], table[1]), TN).reshape(CX, CY, NZ)
        phys[c] = y
        state[c] = jnp.where(fringe, y, farm[c])
        x = modes[pl.ds(3 + c, NZ, stride=CHUNK), :]
        q[...] = dot3(halves(x), (table[0], table[1]), TN).reshape(CX, CY, NZ)
        ylo[c, 1 : CX + 1] = jnp.where(fringe, q[:, 0:2], fylo[c, 1 : CX + 1])
        yhi[c, 1 : CX + 1] = jnp.where(fringe, q[:, 2:4], fyhi[c, 1 : CX + 1])
        ylo[c, 0] = jnp.where(below, q[6, 4:6], fylo[c, 0])
        yhi[c, 0] = jnp.where(below, q[6, 6:8], fyhi[c, 0])
        ylo[c, CX + 1] = jnp.where(above, q[10, 4:6], fylo[c, CX + 1])
        yhi[c, CX + 1] = jnp.where(above, q[10, 6:8], fyhi[c, CX + 1])
        for i in range(2):
            for half in range(2):
                lines = slice(4 * half, 4 * half + 4)
                xlo[c, i, lines] = jnp.where(below, q[4 * i + half, 4:8], fxlo[c, i, lines])
                xhi[c, i, lines] = jnp.where(above, q[8 + 4 * i + half, 4:8], fxhi[c, i, lines])


def slot_force(u, index):
    column = index[0:1, :]
    level = index[1:2, :]
    turbine = index[2:3, :]
    at_column = jnp.where(
        lax.broadcasted_iota(jnp.int32, (CX * CY, SLOTS), 0) == column, 1.0, 0.0
    ).astype(BF)
    at_level = lax.broadcasted_iota(jnp.int32, (NZ, SLOTS), 0) == level
    owned = jnp.where(lax.broadcasted_iota(jnp.int32, (TURB, SLOTS), 0) == turbine, 1.0, 0.0)
    one = functools.partial(lax.dot_general, preferred_element_type=F32)
    picked = sum(one(part, at_column, dimension_numbers=(TN, ((), ()))) for part in thirds(u))
    values = jnp.sum(jnp.where(at_level, picked, 0.0), axis=0, keepdims=True) + WIND
    sums = jnp.sum(owned * values, axis=1, keepdims=True)
    counts = jnp.sum(owned, axis=1, keepdims=True)
    mean = sums / jnp.maximum(counts, 1.0)
    thrust = -0.5 * THRUST * mean * jnp.abs(mean)
    per_slot = jnp.sum(owned * thrust, axis=0, keepdims=True)
    parts = thirds(jnp.where(at_level, per_slot, 0.0))
    return sum(one(at_column, part, dimension_numbers=(NT, ((), ()))) for part in parts)


EXT = 16
OFF = 4
DIAGONAL = 0.5 * SMAG * SMAG
CROSS = 0.25 * SMAG * SMAG


def force_kernel(cur, index, force):
    force[...] = slot_force(cur[...].reshape(CX * CY, NZ), index).reshape(CX, CY, NZ)


def after_y(x):
    return pltpu.roll(x, EXT - 1, 0)


def before_y(x):
    return pltpu.roll(x, 1, 0)


def after_z(x):
    return pltpu.roll(x, LANES - 1, 1)


def before_z(x):
    return pltpu.roll(x, 1, 1)


def assemble(s, cur, xlo, xhi, ylo, yhi, begin, end):
    for c in range(3):
        s[c, begin:end] = jnp.zeros((end - begin, EXT, LANES), F32)
        own = slice(max(begin, 2), min(end, CX + 2))
        s[c, own, OFF : OFF + CY, :NZ] = cur[c, own.start - 2 : own.stop - 2]
        if begin < 2:
            s[c, begin:2, OFF : OFF + CY, :NZ] = xlo[c, begin:2]
        if end > CX + 2:
            s[c, CX + 2 : end, OFF : OFF + CY, :NZ] = xhi[c, : end - CX - 2]
        near = slice(max(begin, 1), min(end, CX + 3))
        s[c, near, OFF - 2 : OFF, :NZ] = ylo[c, near.start - 1 : near.stop - 1]
        s[c, near, OFF + CY : OFF + CY + 2, :NZ] = yhi[c, near.start - 1 : near.stop - 1]


def viscosity(s, e, p):
    f = [s[c, p] for c in range(3)]
    dx = [s[c, p + 1] - s[c, p - 1] for c in range(3)]
    dy = [after_y(f[c]) - before_y(f[c]) for c in range(3)]
    dz = [after_z(f[c]) - before_z(f[c]) for c in range(3)]
    uv = dy[0] + dx[1]
    uw = dz[0] + dx[2]
    vw = dz[1] + dy[2]
    e[p] = jnp.sqrt(
        DIAGONAL * (dx[0] * dx[0] + dy[1] * dy[1] + dz[2] * dz[2])
        + CROSS * (uv * uv + uw * uw + vw * vw)
    )


def fluxes(speed, eddy, fa, fb):
    speed = 0.25 * speed
    eddy = 0.5 * eddy
    plus = speed + eddy
    minus = speed - eddy
    return [plus * fa[c] + minus * fb[c] for c in range(3)]


def face(s, e, p):
    fa = [s[c, p] for c in range(3)]
    fb = [s[c, p + 1] for c in range(3)]
    return fluxes(fa[0] + fb[0] + 2.0 * WIND, e[p] + e[p + 1], fa, fb)


def advance(alpha, beta, s, e, force, base, store, p, below):
    f = [s[c, p] for c in range(3)]
    eddy = e[p]
    above = face(s, e, p)
    fy = [after_y(f[c]) for c in range(3)]
    along_y = fluxes(f[1] + fy[1], eddy + after_y(eddy), f, fy)
    fz = [after_z(f[c]) for c in range(3)]
    along_z = fluxes(f[2] + fz[2], eddy + after_z(eddy), f, fz)
    for c in range(3):
        rate = (
            below[c]
            - above[c]
            + (before_y(along_y[c]) - along_y[c])
            + (before_z(along_z[c]) - along_z[c])
        )
        value = (beta * (f[c] + STEP * rate))[OFF : OFF + CY, :NZ]
        if c == 0:
            value = value + (beta * STEP) * force[p - 2]
        if alpha != 0.0:
            value = value + alpha * base[c, p - 2]
        store(c, p - 2, value)
    return above


def edge_kernel(alpha, beta, cur, xlo, xhi, ylo, yhi, base, force, low, high, s, e):
    assemble(s, cur, xlo, xhi, ylo, yhi, 0, 6)
    assemble(s, cur, xlo, xhi, ylo, yhi, CX - 2, CX + 4)
    for start, out in ((2, low), (CX, high)):
        for p in range(start - 1, start + 3):
            viscosity(s, e, p)

        def store(c, x, value, out=out, start=start):
            out[c, x + 2 - start] = value

        below = face(s, e, start - 1)
        for p in (start, start + 1):
            below = advance(alpha, beta, s, e, force, base, store, p, below)


GROUP = 4


def whole_kernel(
    alpha, beta, cur, xlo, xhi, ylo, yhi, base, force, other, out, kept, s, e, new, done, sent
):
    copies = [pltpu.make_async_copy(other, kept, done)]
    copies[0].start()
    assemble(s, cur, xlo, xhi, ylo, yhi, 0, CX + 4)

    for p in range(1, CX + 3):
        viscosity(s, e, p)

    def store(c, x, value):
        new[c, x] = value

    below = face(s, e, 1)
    for p in range(2, CX + 2):
        below = advance(alpha, beta, s, e, force, base, store, p, below)
        if (p - 1) % GROUP == 0:
            planes = slice(p - 1 - GROUP, p - 1)
            copies.append(
                pltpu.make_async_copy(new.at[:, planes], out.at[:, planes], sent.at[p // GROUP - 1])
            )
            copies[-1].start()
    for copy in copies:
        copy.wait()


def inner_kernel(alpha, beta, cur, xlo, xhi, ylo, yhi, base, force, low, high, new, s, e):
    assemble(s, cur, xlo, xhi, ylo, yhi, 2, CX + 2)

    for p in range(3, CX + 1):
        viscosity(s, e, p)

    def store(c, x, value):
        new[c, x] = value

    below = face(s, e, 3)
    for p in range(4, CX):
        below = advance(alpha, beta, s, e, force, base, store, p, below)
    for c in range(3):
        new[c, :2] = low[c]
        new[c, CX - 2 :] = high[c]


def sds(*shape):
    return jax.ShapeDtypeStruct(shape, F32)


def cost(micros):
    return pl.CostEstimate(flops=1000000 * micros, bytes_accessed=3000000 * micros, transcendentals=0)


VM = pl.BlockSpec(memory_space=pltpu.VMEM)
SM = pl.BlockSpec(memory_space=pltpu.SMEM)
LIMIT = pltpu.CompilerParams(vmem_limit_bytes=48 << 20)


def exchange(value):
    whole = value.reshape(ROWS * COLS, 1, -1)
    whole = lax.all_to_all(whole, ("gx", "gy"), 0, 0, tiled=True)
    return whole.reshape(value.shape)


def halo_x(low, high):
    return ring(high, "gx", 1), ring(low, "gx", -1)


def halo_y(current, xlo, xhi):
    first = jnp.concatenate([xlo[:, 1:, :2], current[:, :, :2], xhi[:, :1, :2]], axis=1)
    last = jnp.concatenate(
        [xlo[:, 1:, CY - 2 :], current[:, :, CY - 2 :], xhi[:, :1, CY - 2 :]], axis=1
    )
    return first, last


def ring(value, axis, steps):
    count = lax.axis_size(axis)
    return lax.ppermute(value, axis, [(i, (i + steps) % count) for i in range(count)])


def shards(farm_velocity, precursor_velocity, turb_cell, turb_slot, disk_mask):
    row = lax.axis_index("gx")
    column = lax.axis_index("gy")
    centre, face = (jnp.asarray(t) for t in vertical_tables())
    tables = [jnp.asarray(t) for t in plane_tables()]
    order = (row * COLS + column).astype(F32)
    rise = (2.0 * jnp.sin(order * (math.pi / (2 * NZ)))).reshape(1, 1)
    with jax.named_scope("vertical_modes"):
        modes = pl.pallas_call(
            modes_kernel,
            out_shape=sds(3 * ROWS * COLS, CX * CY),
            in_specs=[pl.BlockSpec(memory_space=pltpu.HBM)] * 3,
            out_specs=VM,
            scratch_shapes=[
                pltpu.VMEM((3, CX, CY, NZ), F32),
                pltpu.VMEM((2, NZ, NZ), BF),
                pltpu.VMEM((2, NZ, NZ), BF),
                pltpu.SemaphoreType.DMA((5,)),
            ],
            compiler_params=pltpu.CompilerParams(vmem_limit_bytes=60 << 20),
        )(precursor_velocity, centre, face)
        modes, farm_velocity = lax.optimization_barrier((modes, farm_velocity))
        modes = exchange(modes)
    with jax.named_scope("farm_halo_x"):
        fxlo, fxhi = halo_x(farm_velocity[:, :2], farm_velocity[:, CX - 2 :])
        first, last = halo_y(farm_velocity, fxlo, fxhi)
    with jax.named_scope("planes"):
        modes = pl.pallas_call(
            plane_kernel,
            out_shape=sds(CHUNK * ROWS * COLS, CX * CY),
            in_specs=[SM] + [VM] * 6,
            out_specs=VM,
            compiler_params=LIMIT,
        )(rise, modes, *tables)
        modes, first, last = lax.optimization_barrier((modes, first, last))
        modes = exchange(modes)
    with jax.named_scope("farm_halo_y"):
        fylo, fyhi = ring(last, "gy", 1), ring(first, "gy", -1)
    with jax.named_scope("levels"):
        phys, state, xlo, xhi, ylo, yhi = pl.pallas_call(
            levels_kernel,
            out_shape=(sds(3, CX, CY, NZ),) * 2 + (sds(3, 2, CY, NZ),) * 2 + (sds(3, CX + 2, 2, NZ),) * 2,
            in_specs=[SM] + [VM] * 8,
            out_specs=(VM,) * 6,
            scratch_shapes=[pltpu.VMEM((CX, CY, NZ), F32)],
            compiler_params=LIMIT,
        )(row.reshape(1).astype(jnp.int32), modes, farm_velocity, fxlo, fxhi, fylo, fyhi, centre, face)
    cell = turb_cell.reshape(1, SLOTS)
    slot = jnp.where(disk_mask.reshape(1, SLOTS) == 1, turb_slot.reshape(1, SLOTS), -1)
    index = jnp.concatenate([cell // NZ, cell % NZ, slot, jnp.zeros((5, SLOTS), jnp.int32)], axis=0)

    current = state
    weights = ((0.0, 1.0), (0.75, 0.25), (1.0 / 3.0, 2.0 / 3.0))
    for section, (alpha, beta) in enumerate(weights):
        with jax.named_scope("drag"):
            force = pl.pallas_call(
                force_kernel,
                grid=(1,),
                out_shape=sds(CX, CY, NZ),
                in_specs=[
                    pl.BlockSpec((None, CX, CY, NZ), lambda i: (0, 0, 0, 0)),
                    pl.BlockSpec((8, SLOTS), lambda i: (0, 0)),
                ],
                out_specs=pl.BlockSpec((CX, CY, NZ), lambda i: (0, 0, 0)),
                compiler_params=LIMIT,
                cost_estimate=cost(1),
            )(current, index)
        if section > 0:
            with jax.named_scope("halo"):
                xlo, xhi = halo_x(low, high)
                if section == 1:
                    phys, xlo, xhi = lax.optimization_barrier((phys, xlo, xhi))
                    precursor_new = lax.ppermute(phys, "gx", [(home(i), i) for i in range(ROWS)])
                first, last = halo_y(current, xlo, xhi)
                ylo, yhi = ring(last, "gy", 1), ring(first, "gy", -1)
        scratch = [
            pltpu.VMEM((3, CX + 4, EXT, LANES), F32),
            pltpu.VMEM((CX + 4, EXT, LANES), F32),
        ]
        operands = (current, xlo, xhi, ylo, yhi, state, force)
        if section == 2:
            with jax.named_scope("whole"):
                current, precursor_new = pl.pallas_call(
                    functools.partial(whole_kernel, alpha, beta),
                    out_shape=(sds(3, CX, CY, NZ),) * 2,
                    in_specs=[VM] * 7 + [pl.BlockSpec(memory_space=pl.ANY)],
                    out_specs=(pl.BlockSpec(memory_space=pl.ANY),) * 2,
                    scratch_shapes=scratch
                    + [
                        pltpu.VMEM((3, CX, CY, NZ), F32),
                        pltpu.SemaphoreType.DMA,
                        pltpu.SemaphoreType.DMA((CX // GROUP,)),
                    ],
                    compiler_params=LIMIT,
                    cost_estimate=cost(5),
                )(*operands, precursor_new)
            break
        with jax.named_scope("edge"):
            low, high = pl.pallas_call(
                functools.partial(edge_kernel, alpha, beta),
                out_shape=(sds(3, 2, CY, NZ),) * 2,
                in_specs=[VM] * 7,
                out_specs=(VM,) * 2,
                scratch_shapes=scratch,
                compiler_params=LIMIT,
                cost_estimate=cost(2),
            )(*operands)
        if section == 0:
            low, high, state = lax.optimization_barrier((low, high, state))
            operands = operands[:5] + (state, force)
        with jax.named_scope("inner"):
            current = pl.pallas_call(
                functools.partial(inner_kernel, alpha, beta),
                out_shape=sds(3, CX, CY, NZ),
                in_specs=[VM] * 9,
                out_specs=VM,
                scratch_shapes=scratch,
                compiler_params=LIMIT,
                cost_estimate=cost(4),
            )(*operands, low, high)
    return current, precursor_new


def solution(mesh):
    return jax.shard_map(
        shards,
        mesh=mesh,
        in_specs=(
            P(None, "gx", "gy", None),
            P(None, "gx", "gy", None),
            P("gx", "gy", None),
            P("gx", "gy", None),
            P("gx", "gy", None),
        ),
        out_specs=(P(None, "gx", "gy", None), P(None, "gx", "gy", None)),
        check_vma=False,
    )
```

```python
import functools
import math

import jax
import jax.numpy as jnp
import ml_dtypes
import numpy as np
from jax import lax
from jax.experimental import pallas as pl
from jax.experimental.pallas import tpu as pltpu
from jax.sharding import PartitionSpec as P

NF = 48
TURB = 16
WIND = 3.0
STEP = 0.1
SMAG = 0.0289
THRUST = 1.33
DIFFUSE = 0.05

CX, CY, NZ = 16, 8, 192
NX, NY = 256, 128
ROWS, COLS = 16, 16
SLOTS = 256
FRINGE = NF // CX
LANES = 256

BF = jnp.bfloat16
F32 = jnp.float32


def split(table):
    table = np.asarray(table, np.float64)
    high = table.astype(np.float32).astype(ml_dtypes.bfloat16)
    low = (table - high.astype(np.float64)).astype(np.float32).astype(ml_dtypes.bfloat16)
    return np.stack([high, low])


def vertical_tables():
    height = np.arange(NZ)[None, :]
    order = np.arange(NZ)[:, None]
    scale = np.where(order == 0, math.sqrt(1.0 / NZ), math.sqrt(2.0 / NZ))
    centre = scale * np.cos(math.pi / (2 * NZ) * (order * (2 * height + 1) % (4 * NZ)))
    keep = (height < NZ - 1) & (order > 0)
    face = math.sqrt(2.0 / NZ) * np.sin(math.pi / NZ * (order * (height + 1) % (2 * NZ))) * keep
    return split(centre), split(face)


def home(row):
    if row < FRINGE:
        return row + ROWS - FRINGE
    if row >= ROWS - FRINGE:
        return row - (ROWS - FRINGE)
    return row


def plane_tables():
    half = NX // 2
    angle = 2.0 * math.pi / NX * (np.arange(half)[:, None] * np.arange(NX)[None, :] % NX)
    forward_x = np.concatenate([np.cos(angle), -np.sin(angle)], axis=0)
    weight = np.where(np.arange(half) == 0, 1.0, 2.0)[:, None] / NX
    inverse_x = np.concatenate([np.cos(angle) * weight, -np.sin(angle) * weight], axis=0).T
    order = np.concatenate([np.arange(CX) + CX * home(row) for row in range(ROWS)])
    places = (CX * np.arange(ROWS)[:, None] + np.array([-2, -1, CX, CX + 1])[None, :]) % NX
    source = np.where(places < NF, NX - NF + places, 0)
    beside = inverse_x[np.repeat(source.reshape(-1), 4)]
    inverse_x = inverse_x[order]
    angle = 2.0 * math.pi / NY * (np.arange(NY)[:, None] * np.arange(NY)[None, :] % NY)
    keep = (np.arange(NY) != NY // 2)[None, :]
    forward_y = np.concatenate([np.cos(angle) * keep, np.sin(angle) * keep], axis=1)
    inverse_y = np.concatenate([np.cos(angle), np.sin(angle)], axis=1) / NY
    return split(np.concatenate([forward_x, inverse_x, beside, forward_y, inverse_y], axis=0))


def halves(x):
    high = x.astype(BF)
    low = (x - high.astype(F32)).astype(BF)
    return high, low


def thirds(x):
    high, rest = x.astype(BF), x
    rest = rest - high.astype(F32)
    middle = rest.astype(BF)
    rest = rest - middle.astype(F32)
    return rest.astype(BF), middle, high


def dot3(a, b, dims):
    one = functools.partial(lax.dot_general, dimension_numbers=(dims, ((), ())), preferred_element_type=F32)
    return one(a[0], b[0]) + (one(a[0], b[1]) + one(a[1], b[0]))


NN = ((1,), (0,))
NT = ((1,), (1,))
TN = ((0,), (0,))


def modes_kernel(field_hbm, centre_hbm, face_hbm, out, field, centre, face, done):
    copies = [
        pltpu.make_async_copy(centre_hbm, centre, done.at[0]),
        pltpu.make_async_copy(field_hbm.at[0], field.at[0], done.at[1]),
        pltpu.make_async_copy(field_hbm.at[1], field.at[1], done.at[2]),
        pltpu.make_async_copy(face_hbm, face, done.at[3]),
        pltpu.make_async_copy(field_hbm.at[2], field.at[2], done.at[4]),
    ]
    for copy in copies:
        copy.start()
    out[3 * NZ :, :] = jnp.zeros((3 * (ROWS * COLS - NZ), CX * CY), F32)
    for c, ready in ((0, copies[:2]), (1, copies[2:3]), (2, copies[3:])):
        for copy in ready:
            copy.wait()
        table = face if c == 2 else centre
        x = field[c].reshape(CX * CY, NZ)
        out[pl.ds(c, NZ, stride=3), :] = dot3((table[0], table[1]), halves(x), NT)


def swap_masks():
    row = lax.broadcasted_iota(jnp.int32, (8, CX * CY), 0)
    lane = lax.broadcasted_iota(jnp.int32, (8, CX * CY), 1)
    masks = []
    for bit in range(3):
        row_bit = (row >> bit) & 1
        lane_bit = (lane >> (3 + bit)) & 1
        masks.append(((row_bit < lane_bit), (row_bit > lane_bit), row_bit == 0))
    return masks, lane >= 64


def swapped(parts, masks):
    masks, upper = masks
    low, high = parts
    low, high = (
        jnp.where(upper, pltpu.roll(high, 64, 1), low),
        jnp.where(upper, high, pltpu.roll(low, 64, 1)),
    )
    out = []
    for x in (low, high):
        for bit in range(3):
            later, earlier, even = masks[bit]
            by_row, by_lane = 1 << bit, 8 << bit
            other = pltpu.roll(x, by_row, 0)
            if by_row != 4:
                other = jnp.where(even, pltpu.roll(x, 8 - by_row, 0), other)
            x = jnp.where(
                later,
                pltpu.roll(other, by_lane, 1),
                jnp.where(earlier, pltpu.roll(other, CX * CY - by_lane, 1), x),
            )
        out.append(x)
    return out


CHUNK = 6


def halo_slots(own, near):
    part = lax.broadcasted_iota(jnp.int32, own.shape, 0) % 4
    slot = lax.broadcasted_iota(jnp.int32, own.shape, 1) % 8
    across = jnp.where(slot < 2, pltpu.roll(own, 2, 1), pltpu.roll(own, 122, 1))
    corner = jnp.where(slot < 6, pltpu.roll(near, 6, 1), pltpu.roll(near, 126, 1))
    along = jnp.where(part == 0, pltpu.roll(near, 4, 1), jnp.where(part == 1, near, corner))
    return jnp.where(slot < 4, across, along)


def plane_kernel(rise_ref, inp, tables, out):
    bounds = (0, NX, 2 * NX, 3 * NX, 3 * NX + NY, 3 * NX + 2 * NY)
    fx, ix, ix2, fy, iy = (
        tuple(tables[part, bounds[i] : bounds[i + 1]] for part in range(2)) for i in range(5)
    )
    half = NX // 2
    masks = swap_masks()
    spec = []
    for c in range(3):
        rows = []
        for r in range(2 * ROWS):
            rows.append(inp[pl.ds(24 * r + c, 8, stride=3), :])
            if r % 2 == 1:
                rows[-2:] = swapped(rows[-2:], masks)
        x = jnp.concatenate(rows, axis=0)
        along = dot3((fx[0], fx[1]), halves(x), NN)
        both = dot3(halves(along), (fy[0], fy[1]), NN)
        re = both[:half, :NY] + both[half:, NY:]
        im = both[half:, :NY] - both[:half, NY:]
        spec.append((re, im))
    rise = rise_ref[0, 0]
    k = lax.broadcasted_iota(jnp.int32, (half, NY), 0)
    q = lax.broadcasted_iota(jnp.int32, (half, NY), 1)
    kx = (2.0 * math.pi / NX) * k.astype(F32)
    ky = (2.0 * math.pi / NY) * jnp.where(q < NY // 2, q, q - NY).astype(F32)
    hor = kx * kx + ky * ky
    bound = hor + rise * rise
    inverse = jnp.where(bound > 0.0, -1.0 / jnp.where(bound > 0.0, bound, 1.0), 0.0)
    decay = jnp.exp(-DIFFUSE * hor)
    (ur, ui), (vr, vi), (wr, wi) = spec
    press_re = (rise * wr - kx * ui - ky * vi) * inverse
    press_im = (rise * wi + kx * ur + ky * vr) * inverse
    new = (
        ((ur + kx * press_im) * decay, (ui - kx * press_re) * decay),
        ((vr + ky * press_im) * decay, (vi - ky * press_re) * decay),
        ((wr + rise * press_re) * decay, (wi + rise * press_im) * decay),
    )
    for c in range(3):
        both = dot3(halves(jnp.concatenate(new[c], axis=0)), (iy[0], iy[1]), NN)
        re = both[:half, :NY] - both[half:, NY:]
        im = both[:half, NY:] + both[half:, :NY]
        lines = halves(jnp.concatenate([re, im], axis=0))
        x = dot3((ix[0], ix[1]), lines, NN)
        near = dot3((ix2[0], ix2[1]), lines, NN)
        for r in range(ROWS):
            here = [slice(16 * r + 8 * side, 16 * r + 8 * side + 8) for side in range(2)]
            own = [x[rows] for rows in here]
            pair = swapped(own, masks)
            halo = swapped([halo_slots(own[side], near[here[side]]) for side in range(2)], masks)
            for side in range(2):
                first = CHUNK * (16 * r + 8 * side)
                out[pl.ds(first + c, 8, stride=CHUNK), :] = pair[side]
                out[pl.ds(first + 3 + c, 8, stride=CHUNK), :] = halo[side]


def levels_kernel(
    row_ref, modes, farm, fxlo, fxhi, fylo, fyhi, centre, face, index,
    phys, state, xlo, xhi, ylo, yhi, force, q,
):
    row = row_ref[0]
    fringe = row < FRINGE
    below = (row >= 1) & (row <= FRINGE)
    above = (row < FRINGE - 1) | (row == ROWS - 1)
    for c in range(3):
        table = face if c == 2 else centre
        x = modes[pl.ds(c, NZ, stride=CHUNK), :]
        y = dot3(halves(x), (table[0], table[1]), TN).reshape(CX, CY, NZ)
        phys[c] = y
        state[c] = jnp.where(fringe, y, farm[c])
        if c == 0:
            force[...] = slot_force(state[0].reshape(CX * CY, NZ), index).reshape(CX, CY, NZ)
        x = modes[pl.ds(3 + c, NZ, stride=CHUNK), :]
        q[...] = dot3(halves(x), (table[0], table[1]), TN).reshape(CX, CY, NZ)
        ylo[c, 1 : CX + 1] = jnp.where(fringe, q[:, 0:2], fylo[c])
        yhi[c, 1 : CX + 1] = jnp.where(fringe, q[:, 2:4], fyhi[c])
        ylo[c, 0] = jnp.where(below, q[6, 4:6], fxlo[c, 1, 0:2])
        yhi[c, 0] = jnp.where(below, q[6, 6:8], fxlo[c, 1, CY + 2 :])
        ylo[c, CX + 1] = jnp.where(above, q[10, 4:6], fxhi[c, 0, 0:2])
        yhi[c, CX + 1] = jnp.where(above, q[10, 6:8], fxhi[c, 0, CY + 2 :])
        for i in range(2):
            for half in range(2):
                lines = slice(4 * half, 4 * half + 4)
                wide = slice(4 * half + 2, 4 * half + 6)
                xlo[c, i, lines] = jnp.where(below, q[4 * i + half, 4:8], fxlo[c, i, wide])
                xhi[c, i, lines] = jnp.where(above, q[8 + 4 * i + half, 4:8], fxhi[c, i, wide])


def slot_force(u, index):
    column = index[0:1, :]
    level = index[1:2, :]
    turbine = index[2:3, :]
    at_column = jnp.where(
        lax.broadcasted_iota(jnp.int32, (CX * CY, SLOTS), 0) == column, 1.0, 0.0
    ).astype(BF)
    at_level = lax.broadcasted_iota(jnp.int32, (NZ, SLOTS), 0) == level
    owned = jnp.where(lax.broadcasted_iota(jnp.int32, (TURB, SLOTS), 0) == turbine, 1.0, 0.0)
    one = functools.partial(lax.dot_general, preferred_element_type=F32)
    picked = sum(one(part, at_column, dimension_numbers=(TN, ((), ()))) for part in thirds(u))
    values = jnp.sum(jnp.where(at_level, picked, 0.0), axis=0, keepdims=True) + WIND
    sums = jnp.sum(owned * values, axis=1, keepdims=True)
    counts = jnp.sum(owned, axis=1, keepdims=True)
    mean = sums / jnp.maximum(counts, 1.0)
    thrust = -0.5 * THRUST * mean * jnp.abs(mean)
    per_slot = jnp.sum(owned * thrust, axis=0, keepdims=True)
    parts = thirds(jnp.where(at_level, per_slot, 0.0))
    return sum(one(at_column, part, dimension_numbers=(NT, ((), ()))) for part in parts)


EXT = 16
OFF = 4
DIAGONAL = 0.5 * SMAG * SMAG
CROSS = 0.25 * SMAG * SMAG


def force_kernel(cur, index, force):
    force[...] = slot_force(cur[...].reshape(CX * CY, NZ), index).reshape(CX, CY, NZ)


def after_y(x):
    return pltpu.roll(x, EXT - 1, 0)


def before_y(x):
    return pltpu.roll(x, 1, 0)


def after_z(x):
    return pltpu.roll(x, LANES - 1, 1)


def before_z(x):
    return pltpu.roll(x, 1, 1)


def assemble(s, cur, xlo, xhi, ylo, yhi, begin, end):
    for c in range(3):
        s[c, begin:end] = jnp.zeros((end - begin, EXT, LANES), F32)
        own = slice(max(begin, 2), min(end, CX + 2))
        s[c, own, OFF : OFF + CY, :NZ] = cur[c, own.start - 2 : own.stop - 2]
        if begin < 2:
            s[c, begin:2, OFF : OFF + CY, :NZ] = xlo[c, begin:2]
        if end > CX + 2:
            s[c, CX + 2 : end, OFF : OFF + CY, :NZ] = xhi[c, : end - CX - 2]
        near = slice(max(begin, 1), min(end, CX + 3))
        s[c, near, OFF - 2 : OFF, :NZ] = ylo[c, near.start - 1 : near.stop - 1]
        s[c, near, OFF + CY : OFF + CY + 2, :NZ] = yhi[c, near.start - 1 : near.stop - 1]


def viscosity(s, e, p):
    f = [s[c, p] for c in range(3)]
    dx = [s[c, p + 1] - s[c, p - 1] for c in range(3)]
    dy = [after_y(f[c]) - before_y(f[c]) for c in range(3)]
    dz = [after_z(f[c]) - before_z(f[c]) for c in range(3)]
    uv = dy[0] + dx[1]
    uw = dz[0] + dx[2]
    vw = dz[1] + dy[2]
    e[p] = jnp.sqrt(
        DIAGONAL * (dx[0] * dx[0] + dy[1] * dy[1] + dz[2] * dz[2])
        + CROSS * (uv * uv + uw * uw + vw * vw)
    )


def fluxes(speed, eddy, fa, fb):
    speed = 0.25 * speed
    eddy = 0.5 * eddy
    plus = speed + eddy
    minus = speed - eddy
    return [plus * fa[c] + minus * fb[c] for c in range(3)]


def face(s, e, p):
    own = slice(OFF, OFF + CY)
    fa = [s[c, p, own, :] for c in range(3)]
    fb = [s[c, p + 1, own, :] for c in range(3)]
    return fluxes(fa[0] + fb[0] + 2.0 * WIND, e[p, own, :] + e[p + 1, own, :], fa, fb)


def advance(alpha, beta, s, e, force, base, store, p, below):
    own, later, earlier = (slice(OFF + step, OFF + step + CY) for step in (0, 1, -1))
    f = [s[c, p, own, :] for c in range(3)]
    eddy = e[p, own, :]
    above = face(s, e, p)
    fy = [s[c, p, later, :] for c in range(3)]
    left_y = fluxes(f[1] + fy[1], eddy + e[p, later, :], f, fy)
    fy = [s[c, p, earlier, :] for c in range(3)]
    right_y = fluxes(f[1] + fy[1], eddy + e[p, earlier, :], fy, f)
    fz = [after_z(f[c]) for c in range(3)]
    along_z = fluxes(f[2] + fz[2], eddy + after_z(eddy), f, fz)
    for c in range(3):
        rate = (
            (below[c] - above[c])
            + (right_y[c] - left_y[c])
            + (before_z(along_z[c]) - along_z[c])
        )
        value = (beta * (f[c] + STEP * rate))[:, :NZ]
        if c == 0:
            value = value + (beta * STEP) * force[p - 2]
        if alpha != 0.0:
            value = value + alpha * base[c, p - 2]
        store(c, p - 2, value)
    return above


def edge_kernel(alpha, beta, cur, xlo, xhi, ylo, yhi, base, force, low, high, s, e):
    assemble(s, cur, xlo, xhi, ylo, yhi, 0, 6)
    assemble(s, cur, xlo, xhi, ylo, yhi, CX - 2, CX + 4)
    for start, out in ((2, low), (CX, high)):
        for p in range(start - 1, start + 3):
            viscosity(s, e, p)

        def store(c, x, value, out=out, start=start):
            out[c, x + 2 - start] = value

        below = face(s, e, start - 1)
        for p in (start, start + 1):
            below = advance(alpha, beta, s, e, force, base, store, p, below)


GROUP = 4


def whole_kernel(
    alpha, beta, cur, xlo, xhi, ylo, yhi, base, force, other, out, kept, s, e, new, done, sent
):
    copies = [pltpu.make_async_copy(other, kept, done)]
    copies[0].start()
    assemble(s, cur, xlo, xhi, ylo, yhi, 0, CX + 4)

    for p in range(1, CX + 3):
        viscosity(s, e, p)

    def store(c, x, value):
        new[c, x] = value

    below = face(s, e, 1)
    for p in range(2, CX + 2):
        below = advance(alpha, beta, s, e, force, base, store, p, below)
        if (p - 1) % GROUP == 0:
            planes = slice(p - 1 - GROUP, p - 1)
            copies.append(
                pltpu.make_async_copy(new.at[:, planes], out.at[:, planes], sent.at[p // GROUP - 1])
            )
            copies[-1].start()
    for copy in copies:
        copy.wait()


def inner_kernel(alpha, beta, cur, xlo, xhi, ylo, yhi, base, force, low, high, new, s, e):
    assemble(s, cur, xlo, xhi, ylo, yhi, 2, CX + 2)

    for p in range(3, CX + 1):
        viscosity(s, e, p)

    def store(c, x, value):
        new[c, x] = value

    below = face(s, e, 3)
    for p in range(4, CX):
        below = advance(alpha, beta, s, e, force, base, store, p, below)
    for c in range(3):
        new[c, :2] = low[c]
        new[c, CX - 2 :] = high[c]


def sds(*shape):
    return jax.ShapeDtypeStruct(shape, F32)


def cost(micros):
    return pl.CostEstimate(flops=1000000 * micros, bytes_accessed=3000000 * micros, transcendentals=0)


VM = pl.BlockSpec(memory_space=pltpu.VMEM)
SM = pl.BlockSpec(memory_space=pltpu.SMEM)
LIMIT = pltpu.CompilerParams(vmem_limit_bytes=48 << 20)


def exchange(value):
    whole = value.reshape(ROWS * COLS, 1, -1)
    whole = lax.all_to_all(whole, ("gx", "gy"), 0, 0, tiled=True)
    return whole.reshape(value.shape)


def halo_x(low, high):
    return ring(high, "gx", 1), ring(low, "gx", -1)


def halo_y(current, xlo, xhi):
    first = jnp.concatenate([xlo[:, 1:, :2], current[:, :, :2], xhi[:, :1, :2]], axis=1)
    last = jnp.concatenate(
        [xlo[:, 1:, CY - 2 :], current[:, :, CY - 2 :], xhi[:, :1, CY - 2 :]], axis=1
    )
    return first, last


def ring(value, axis, steps):
    count = lax.axis_size(axis)
    return lax.ppermute(value, axis, [(i, (i + steps) % count) for i in range(count)])


def shards(farm_velocity, precursor_velocity, turb_cell, turb_slot, disk_mask):
    row = lax.axis_index("gx")
    column = lax.axis_index("gy")
    centre, face = (jnp.asarray(t) for t in vertical_tables())
    tables = jnp.asarray(plane_tables())
    order = (row * COLS + column).astype(F32)
    rise = (2.0 * jnp.sin(order * (math.pi / (2 * NZ)))).reshape(1, 1)
    with jax.named_scope("vertical_modes"):
        modes = pl.pallas_call(
            modes_kernel,
            out_shape=sds(3 * ROWS * COLS, CX * CY),
            in_specs=[pl.BlockSpec(memory_space=pltpu.HBM)] * 3,
            out_specs=VM,
            scratch_shapes=[
                pltpu.VMEM((3, CX, CY, NZ), F32),
                pltpu.VMEM((2, NZ, NZ), BF),
                pltpu.VMEM((2, NZ, NZ), BF),
                pltpu.SemaphoreType.DMA((5,)),
            ],
            compiler_params=pltpu.CompilerParams(vmem_limit_bytes=60 << 20),
        )(precursor_velocity, centre, face)
        modes, farm_velocity = lax.optimization_barrier((modes, farm_velocity))
        modes = exchange(modes)
    with jax.named_scope("farm_halo_y"):
        fylo = ring(farm_velocity[:, :, CY - 2 :], "gy", 1)
        fyhi = ring(farm_velocity[:, :, :2], "gy", -1)
        low, high = (
            jnp.concatenate([fylo[:, part], farm_velocity[:, part], fyhi[:, part]], axis=2)
            for part in (slice(0, 2), slice(CX - 2, CX))
        )
    with jax.named_scope("planes"):
        modes = pl.pallas_call(
            plane_kernel,
            out_shape=sds(CHUNK * ROWS * COLS, CX * CY),
            in_specs=[SM] + [VM] * 2,
            out_specs=VM,
            compiler_params=LIMIT,
        )(rise, modes, tables)
        modes, low, high = lax.optimization_barrier((modes, low, high))
        modes = exchange(modes)
    with jax.named_scope("farm_halo_x"):
        fxlo, fxhi = halo_x(low, high)
    cell = turb_cell.reshape(1, SLOTS)
    slot = jnp.where(disk_mask.reshape(1, SLOTS) == 1, turb_slot.reshape(1, SLOTS), -1)
    index = jnp.concatenate([cell // NZ, cell % NZ, slot, jnp.zeros((5, SLOTS), jnp.int32)], axis=0)
    with jax.named_scope("levels"):
        phys, state, xlo, xhi, ylo, yhi, force = pl.pallas_call(
            levels_kernel,
            out_shape=(sds(3, CX, CY, NZ),) * 2
            + (sds(3, 2, CY, NZ),) * 2
            + (sds(3, CX + 2, 2, NZ),) * 2
            + (sds(CX, CY, NZ),),
            in_specs=[SM] + [VM] * 9,
            out_specs=(VM,) * 7,
            scratch_shapes=[pltpu.VMEM((CX, CY, NZ), F32)],
            compiler_params=LIMIT,
        )(row.reshape(1).astype(jnp.int32), modes, farm_velocity, fxlo, fxhi, fylo, fyhi, centre, face, index)
    current = state
    weights = ((0.0, 1.0), (0.75, 0.25), (1.0 / 3.0, 2.0 / 3.0))
    for section, (alpha, beta) in enumerate(weights):
        with jax.named_scope("drag"):
            force = force if section == 0 else pl.pallas_call(
                force_kernel,
                grid=(1,),
                out_shape=sds(CX, CY, NZ),
                in_specs=[
                    pl.BlockSpec((None, CX, CY, NZ), lambda i: (0, 0, 0, 0)),
                    pl.BlockSpec((8, SLOTS), lambda i: (0, 0)),
                ],
                out_specs=pl.BlockSpec((CX, CY, NZ), lambda i: (0, 0, 0)),
                compiler_params=LIMIT,
                cost_estimate=cost(1),
            )(current, index)
        if section > 0:
            with jax.named_scope("halo"):
                xlo, xhi = halo_x(low, high)
                if section == 1:
                    phys, xlo, xhi = lax.optimization_barrier((phys, xlo, xhi))
                    precursor_new = lax.ppermute(phys, "gx", [(home(i), i) for i in range(ROWS)])
                first, last = halo_y(current, xlo, xhi)
                ylo, yhi = ring(last, "gy", 1), ring(first, "gy", -1)
        scratch = [
            pltpu.VMEM((3, CX + 4, EXT, LANES), F32),
            pltpu.VMEM((CX + 4, EXT, LANES), F32),
        ]
        operands = (current, xlo, xhi, ylo, yhi, state, force)
        if section == 2:
            with jax.named_scope("whole"):
                current, precursor_new = pl.pallas_call(
                    functools.partial(whole_kernel, alpha, beta),
                    out_shape=(sds(3, CX, CY, NZ),) * 2,
                    in_specs=[VM] * 7 + [pl.BlockSpec(memory_space=pl.ANY)],
                    out_specs=(pl.BlockSpec(memory_space=pl.ANY),) * 2,
                    scratch_shapes=scratch
                    + [
                        pltpu.VMEM((3, CX, CY, NZ), F32),
                        pltpu.SemaphoreType.DMA,
                        pltpu.SemaphoreType.DMA((CX // GROUP,)),
                    ],
                    compiler_params=LIMIT,
                    cost_estimate=cost(5),
                )(*operands, precursor_new)
            break
        with jax.named_scope("edge"):
            low, high = pl.pallas_call(
                functools.partial(edge_kernel, alpha, beta),
                out_shape=(sds(3, 2, CY, NZ),) * 2,
                in_specs=[VM] * 7,
                out_specs=(VM,) * 2,
                scratch_shapes=scratch,
                compiler_params=LIMIT,
                cost_estimate=cost(2),
            )(*operands)
        if section == 0:
            low, high, state = lax.optimization_barrier((low, high, state))
            operands = operands[:5] + (state, force)
        with jax.named_scope("inner"):
            current = pl.pallas_call(
                functools.partial(inner_kernel, alpha, beta),
                out_shape=sds(3, CX, CY, NZ),
                in_specs=[VM] * 9,
                out_specs=VM,
                scratch_shapes=scratch,
                compiler_params=LIMIT,
                cost_estimate=cost(4),
            )(*operands, low, high)
    return current, precursor_new


def solution(mesh):
    return jax.shard_map(
        shards,
        mesh=mesh,
        in_specs=(
            P(None, "gx", "gy", None),
            P(None, "gx", "gy", None),
            P("gx", "gy", None),
            P("gx", "gy", None),
            P("gx", "gy", None),
        ),
        out_specs=(P(None, "gx", "gy", None), P(None, "gx", "gy", None)),
        check_vma=False,
    )
```

```python
import functools
import math

import jax
import jax.numpy as jnp
import ml_dtypes
import numpy as np
from jax import lax
from jax.experimental import pallas as pl
from jax.experimental.pallas import tpu as pltpu
from jax.sharding import PartitionSpec as P

NF = 48
TURB = 16
WIND = 3.0
STEP = 0.1
SMAG = 0.0289
THRUST = 1.33
DIFFUSE = 0.05

CX, CY, NZ = 16, 8, 192
NX, NY = 256, 128
ROWS, COLS = 16, 16
SLOTS = 256
FRINGE = NF // CX
LANES = 256

BF = jnp.bfloat16
F32 = jnp.float32


def split(table):
    table = np.asarray(table, np.float64)
    high = table.astype(np.float32).astype(ml_dtypes.bfloat16)
    low = (table - high.astype(np.float64)).astype(np.float32).astype(ml_dtypes.bfloat16)
    return np.stack([high, low])


def vertical_tables():
    height = np.arange(NZ)[None, :]
    order = np.arange(NZ)[:, None]
    scale = np.where(order == 0, math.sqrt(1.0 / NZ), math.sqrt(2.0 / NZ))
    centre = scale * np.cos(math.pi / (2 * NZ) * (order * (2 * height + 1) % (4 * NZ)))
    keep = (height < NZ - 1) & (order > 0)
    face = math.sqrt(2.0 / NZ) * np.sin(math.pi / NZ * (order * (height + 1) % (2 * NZ))) * keep
    return split(centre), split(face)


def home(row):
    if row < FRINGE:
        return row + ROWS - FRINGE
    if row >= ROWS - FRINGE:
        return row - (ROWS - FRINGE)
    return row


def plane_tables():
    half = NX // 2
    angle = 2.0 * math.pi / NX * (np.arange(half)[:, None] * np.arange(NX)[None, :] % NX)
    forward_x = np.concatenate([np.cos(angle), -np.sin(angle)], axis=0)
    weight = np.where(np.arange(half) == 0, 1.0, 2.0)[:, None] / NX
    inverse_x = np.concatenate([np.cos(angle) * weight, -np.sin(angle) * weight], axis=0).T
    order = np.concatenate([np.arange(CX) + CX * home(row) for row in range(ROWS)])
    places = (CX * np.arange(ROWS)[:, None] + np.array([-2, -1, CX, CX + 1])[None, :]) % NX
    source = np.where(places < NF, NX - NF + places, 0)
    beside = inverse_x[np.repeat(source.reshape(-1), 4)]
    inverse_x = inverse_x[order]
    angle = 2.0 * math.pi / NY * (np.arange(NY)[:, None] * np.arange(NY)[None, :] % NY)
    keep = (np.arange(NY) != NY // 2)[None, :]
    forward_y = np.concatenate([np.cos(angle) * keep, np.sin(angle) * keep], axis=1)
    inverse_y = np.concatenate([np.cos(angle), np.sin(angle)], axis=1) / NY
    return split(np.concatenate([forward_x, inverse_x, beside, forward_y, inverse_y], axis=0))


def halves(x):
    high = x.astype(BF)
    low = (x - high.astype(F32)).astype(BF)
    return high, low


def thirds(x):
    high, rest = x.astype(BF), x
    rest = rest - high.astype(F32)
    middle = rest.astype(BF)
    rest = rest - middle.astype(F32)
    return rest.astype(BF), middle, high


def dot3(a, b, dims):
    one = functools.partial(lax.dot_general, dimension_numbers=(dims, ((), ())), preferred_element_type=F32)
    return one(a[0], b[0]) + (one(a[0], b[1]) + one(a[1], b[0]))


NN = ((1,), (0,))
NT = ((1,), (1,))
TN = ((0,), (0,))


def modes_kernel(field_hbm, centre_hbm, face_hbm, out, field, centre, face, done):
    copies = [
        pltpu.make_async_copy(centre_hbm, centre, done.at[0]),
        pltpu.make_async_copy(field_hbm.at[0], field.at[0], done.at[1]),
        pltpu.make_async_copy(field_hbm.at[1], field.at[1], done.at[2]),
        pltpu.make_async_copy(face_hbm, face, done.at[3]),
        pltpu.make_async_copy(field_hbm.at[2], field.at[2], done.at[4]),
    ]
    for copy in copies:
        copy.start()
    out[3 * NZ :, :] = jnp.zeros((3 * (ROWS * COLS - NZ), CX * CY), F32)
    for c, ready in ((0, copies[:2]), (1, copies[2:3]), (2, copies[3:])):
        for copy in ready:
            copy.wait()
        table = face if c == 2 else centre
        x = field[c].reshape(CX * CY, NZ)
        out[pl.ds(c, NZ, stride=3), :] = dot3((table[0], table[1]), halves(x), NT)


def swap_masks():
    row = lax.broadcasted_iota(jnp.int32, (8, CX * CY), 0)
    lane = lax.broadcasted_iota(jnp.int32, (8, CX * CY), 1)
    masks = []
    for bit in range(3):
        row_bit = (row >> bit) & 1
        lane_bit = (lane >> (3 + bit)) & 1
        masks.append(((row_bit < lane_bit), (row_bit > lane_bit), row_bit == 0))
    return masks, lane >= 64


def swapped(parts, masks):
    masks, upper = masks
    low, high = parts
    low, high = (
        jnp.where(upper, pltpu.roll(high, 64, 1), low),
        jnp.where(upper, high, pltpu.roll(low, 64, 1)),
    )
    out = []
    for x in (low, high):
        for bit in range(3):
            later, earlier, even = masks[bit]
            by_row, by_lane = 1 << bit, 8 << bit
            other = pltpu.roll(x, by_row, 0)
            if by_row != 4:
                other = jnp.where(even, pltpu.roll(x, 8 - by_row, 0), other)
            x = jnp.where(
                later,
                pltpu.roll(other, by_lane, 1),
                jnp.where(earlier, pltpu.roll(other, CX * CY - by_lane, 1), x),
            )
        out.append(x)
    return out


CHUNK = 6


def halo_slots(own, near):
    part = lax.broadcasted_iota(jnp.int32, own.shape, 0) % 4
    slot = lax.broadcasted_iota(jnp.int32, own.shape, 1) % 8
    across = jnp.where(slot < 2, pltpu.roll(own, 2, 1), pltpu.roll(own, 122, 1))
    corner = jnp.where(slot < 6, pltpu.roll(near, 6, 1), pltpu.roll(near, 126, 1))
    along = jnp.where(part == 0, pltpu.roll(near, 4, 1), jnp.where(part == 1, near, corner))
    return jnp.where(slot < 4, across, along)


def plane_kernel(rise_ref, inp, tables, out):
    bounds = (0, NX, 2 * NX, 3 * NX, 3 * NX + NY, 3 * NX + 2 * NY)
    fx, ix, ix2, fy, iy = (
        tuple(tables[part, bounds[i] : bounds[i + 1]] for part in range(2)) for i in range(5)
    )
    half = NX // 2
    masks = swap_masks()
    spec = []
    for c in range(3):
        rows = []
        for r in range(2 * ROWS):
            rows.append(inp[pl.ds(24 * r + c, 8, stride=3), :])
            if r % 2 == 1:
                rows[-2:] = swapped(rows[-2:], masks)
        x = jnp.concatenate(rows, axis=0)
        along = dot3((fx[0], fx[1]), halves(x), NN)
        both = dot3(halves(along), (fy[0], fy[1]), NN)
        re = both[:half, :NY] + both[half:, NY:]
        im = both[half:, :NY] - both[:half, NY:]
        spec.append((re, im))
    rise = rise_ref[0, 0]
    k = lax.broadcasted_iota(jnp.int32, (half, NY), 0)
    q = lax.broadcasted_iota(jnp.int32, (half, NY), 1)
    kx = (2.0 * math.pi / NX) * k.astype(F32)
    ky = (2.0 * math.pi / NY) * jnp.where(q < NY // 2, q, q - NY).astype(F32)
    hor = kx * kx + ky * ky
    bound = hor + rise * rise
    inverse = jnp.where(bound > 0.0, -1.0 / jnp.where(bound > 0.0, bound, 1.0), 0.0)
    decay = jnp.exp(-DIFFUSE * hor)
    (ur, ui), (vr, vi), (wr, wi) = spec
    press_re = (rise * wr - kx * ui - ky * vi) * inverse
    press_im = (rise * wi + kx * ur + ky * vr) * inverse
    new = (
        ((ur + kx * press_im) * decay, (ui - kx * press_re) * decay),
        ((vr + ky * press_im) * decay, (vi - ky * press_re) * decay),
        ((wr + rise * press_re) * decay, (wi + rise * press_im) * decay),
    )
    for c in range(3):
        both = dot3(halves(jnp.concatenate(new[c], axis=0)), (iy[0], iy[1]), NN)
        re = both[:half, :NY] - both[half:, NY:]
        im = both[:half, NY:] + both[half:, :NY]
        lines = halves(jnp.concatenate([re, im], axis=0))
        x = dot3((ix[0], ix[1]), lines, NN)
        near = dot3((ix2[0], ix2[1]), lines, NN)
        for r in range(ROWS):
            here = [slice(16 * r + 8 * side, 16 * r + 8 * side + 8) for side in range(2)]
            own = [x[rows] for rows in here]
            pair = swapped(own, masks)
            halo = swapped([halo_slots(own[side], near[here[side]]) for side in range(2)], masks)
            for side in range(2):
                first = CHUNK * (16 * r + 8 * side)
                out[pl.ds(first + c, 8, stride=CHUNK), :] = pair[side]
                out[pl.ds(first + 3 + c, 8, stride=CHUNK), :] = halo[side]


def levels_kernel(
    row_ref, modes, farm, fxlo, fxhi, fylo, fyhi, centre, face, index,
    phys, state, xlo, xhi, ylo, yhi, force, q,
):
    row = row_ref[0]
    fringe = row < FRINGE
    below = (row >= 1) & (row <= FRINGE)
    above = (row < FRINGE - 1) | (row == ROWS - 1)
    for c in range(3):
        table = face if c == 2 else centre
        x = modes[pl.ds(c, NZ, stride=CHUNK), :]
        y = dot3(halves(x), (table[0], table[1]), TN).reshape(CX, CY, NZ)
        phys[c] = y
        state[c] = jnp.where(fringe, y, farm[c])
        if c == 0:
            force[...] = slot_force(state[0].reshape(CX * CY, NZ), index).reshape(CX, CY, NZ)
        x = modes[pl.ds(3 + c, NZ, stride=CHUNK), :]
        q[...] = dot3(halves(x), (table[0], table[1]), TN).reshape(CX, CY, NZ)
        ylo[c, 1 : CX + 1] = jnp.where(fringe, q[:, 0:2], fylo[c])
        yhi[c, 1 : CX + 1] = jnp.where(fringe, q[:, 2:4], fyhi[c])
        ylo[c, 0] = jnp.where(below, q[6, 4:6], fxlo[c, 1, 0:2])
        yhi[c, 0] = jnp.where(below, q[6, 6:8], fxlo[c, 1, CY + 2 :])
        ylo[c, CX + 1] = jnp.where(above, q[10, 4:6], fxhi[c, 0, 0:2])
        yhi[c, CX + 1] = jnp.where(above, q[10, 6:8], fxhi[c, 0, CY + 2 :])
        for i in range(2):
            for half in range(2):
                lines = slice(4 * half, 4 * half + 4)
                wide = slice(4 * half + 2, 4 * half + 6)
                xlo[c, i, lines] = jnp.where(below, q[4 * i + half, 4:8], fxlo[c, i, wide])
                xhi[c, i, lines] = jnp.where(above, q[8 + 4 * i + half, 4:8], fxhi[c, i, wide])


def slot_force(u, index):
    column = index[0:1, :]
    level = index[1:2, :]
    turbine = index[2:3, :]
    at_column = jnp.where(
        lax.broadcasted_iota(jnp.int32, (CX * CY, SLOTS), 0) == column, 1.0, 0.0
    ).astype(BF)
    at_level = lax.broadcasted_iota(jnp.int32, (NZ, SLOTS), 0) == level
    owned = jnp.where(lax.broadcasted_iota(jnp.int32, (TURB, SLOTS), 0) == turbine, 1.0, 0.0)
    one = functools.partial(lax.dot_general, preferred_element_type=F32)
    picked = sum(one(part, at_column, dimension_numbers=(TN, ((), ()))) for part in thirds(u))
    values = jnp.sum(jnp.where(at_level, picked, 0.0), axis=0, keepdims=True) + WIND
    sums = jnp.sum(owned * values, axis=1, keepdims=True)
    counts = jnp.sum(owned, axis=1, keepdims=True)
    mean = sums / jnp.maximum(counts, 1.0)
    thrust = -0.5 * THRUST * mean * jnp.abs(mean)
    per_slot = jnp.sum(owned * thrust, axis=0, keepdims=True)
    parts = thirds(jnp.where(at_level, per_slot, 0.0))
    return sum(one(at_column, part, dimension_numbers=(NT, ((), ()))) for part in parts)


EXT = 16
OFF = 4
DIAGONAL = 0.5 * SMAG * SMAG
CROSS = 0.25 * SMAG * SMAG


def force_kernel(cur, index, force):
    force[...] = slot_force(cur[...].reshape(CX * CY, NZ), index).reshape(CX, CY, NZ)


def after_y(x):
    return pltpu.roll(x, EXT - 1, 0)


def before_y(x):
    return pltpu.roll(x, 1, 0)


def after_z(x):
    return pltpu.roll(x, LANES - 1, 1)


def before_z(x):
    return pltpu.roll(x, 1, 1)


def assemble(s, cur, xlo, xhi, ylo, yhi, begin, end):
    for c in range(3):
        s[c, begin:end] = jnp.zeros((end - begin, EXT, LANES), F32)
        own = slice(max(begin, 2), min(end, CX + 2))
        s[c, own, OFF : OFF + CY, :NZ] = cur[c, own.start - 2 : own.stop - 2]
        if begin < 2:
            s[c, begin:2, OFF : OFF + CY, :NZ] = xlo[c, begin:2]
        if end > CX + 2:
            s[c, CX + 2 : end, OFF : OFF + CY, :NZ] = xhi[c, : end - CX - 2]
        near = slice(max(begin, 1), min(end, CX + 3))
        s[c, near, OFF - 2 : OFF, :NZ] = ylo[c, near.start - 1 : near.stop - 1]
        s[c, near, OFF + CY : OFF + CY + 2, :NZ] = yhi[c, near.start - 1 : near.stop - 1]


def viscosity(s, e, p):
    f = [s[c, p] for c in range(3)]
    dx = [s[c, p + 1] - s[c, p - 1] for c in range(3)]
    dy = [after_y(f[c]) - before_y(f[c]) for c in range(3)]
    dz = [after_z(f[c]) - before_z(f[c]) for c in range(3)]
    uv = dy[0] + dx[1]
    uw = dz[0] + dx[2]
    vw = dz[1] + dy[2]
    e[p] = jnp.sqrt(
        DIAGONAL * (dx[0] * dx[0] + dy[1] * dy[1] + dz[2] * dz[2])
        + CROSS * (uv * uv + uw * uw + vw * vw)
    )


def fluxes(speed, eddy, fa, fb):
    speed = 0.25 * speed
    eddy = 0.5 * eddy
    plus = speed + eddy
    minus = speed - eddy
    return [plus * fa[c] + minus * fb[c] for c in range(3)]


def face(s, e, p):
    own = slice(OFF, OFF + CY)
    fa = [s[c, p, own, :] for c in range(3)]
    fb = [s[c, p + 1, own, :] for c in range(3)]
    return fluxes(fa[0] + fb[0] + 2.0 * WIND, e[p, own, :] + e[p + 1, own, :], fa, fb)


def advance(alpha, beta, s, e, force, base, store, p, below):
    own, later, earlier = (slice(OFF + step, OFF + step + CY) for step in (0, 1, -1))
    f = [s[c, p, own, :] for c in range(3)]
    eddy = e[p, own, :]
    above = face(s, e, p)
    fy = [s[c, p, later, :] for c in range(3)]
    left_y = fluxes(f[1] + fy[1], eddy + e[p, later, :], f, fy)
    fy = [s[c, p, earlier, :] for c in range(3)]
    right_y = fluxes(f[1] + fy[1], eddy + e[p, earlier, :], fy, f)
    fz = [after_z(f[c]) for c in range(3)]
    along_z = fluxes(f[2] + fz[2], eddy + after_z(eddy), f, fz)
    for c in range(3):
        rate = (
            (below[c] - above[c])
            + (right_y[c] - left_y[c])
            + (before_z(along_z[c]) - along_z[c])
        )
        value = (beta * (f[c] + STEP * rate))[:, :NZ]
        if c == 0:
            value = value + (beta * STEP) * force[p - 2]
        if alpha != 0.0:
            value = value + alpha * base[c, p - 2]
        store(c, p - 2, value)
    return above


def edge_kernel(alpha, beta, cur, xlo, xhi, ylo, yhi, base, force, low, high, s, e):
    assemble(s, cur, xlo, xhi, ylo, yhi, 0, 6)
    assemble(s, cur, xlo, xhi, ylo, yhi, CX - 2, CX + 4)
    for start, out in ((2, low), (CX, high)):
        for p in range(start - 1, start + 3):
            viscosity(s, e, p)

        def store(c, x, value, out=out, start=start):
            out[c, x + 2 - start] = value

        below = face(s, e, start - 1)
        for p in (start, start + 1):
            below = advance(alpha, beta, s, e, force, base, store, p, below)


GROUP = 4


def whole_kernel(
    alpha, beta, cur, xlo, xhi, ylo, yhi, base, force, other, out, kept, s, e, new, done, sent
):
    copies = [pltpu.make_async_copy(other, kept, done)]
    copies[0].start()
    assemble(s, cur, xlo, xhi, ylo, yhi, 0, CX + 4)

    for p in range(1, CX + 3):
        viscosity(s, e, p)

    def store(c, x, value):
        new[c, x] = value

    below = face(s, e, 1)
    for p in range(2, CX + 2):
        below = advance(alpha, beta, s, e, force, base, store, p, below)
        if (p - 1) % GROUP == 0:
            planes = slice(p - 1 - GROUP, p - 1)
            copies.append(
                pltpu.make_async_copy(new.at[:, planes], out.at[:, planes], sent.at[p // GROUP - 1])
            )
            copies[-1].start()
    for copy in copies:
        copy.wait()


def inner_kernel(alpha, beta, cur, xlo, xhi, ylo, yhi, base, force, low, high, new, s, e):
    assemble(s, cur, xlo, xhi, ylo, yhi, 2, CX + 2)

    for p in range(3, CX + 1):
        viscosity(s, e, p)

    def store(c, x, value):
        new[c, x] = value

    below = face(s, e, 3)
    for p in range(4, CX):
        below = advance(alpha, beta, s, e, force, base, store, p, below)
    for c in range(3):
        new[c, :2] = low[c]
        new[c, CX - 2 :] = high[c]


def sds(*shape):
    return jax.ShapeDtypeStruct(shape, F32)


def cost(micros):
    return pl.CostEstimate(flops=1000000 * micros, bytes_accessed=3000000 * micros, transcendentals=0)


VM = pl.BlockSpec(memory_space=pltpu.VMEM)
SM = pl.BlockSpec(memory_space=pltpu.SMEM)
LIMIT = pltpu.CompilerParams(vmem_limit_bytes=48 << 20)


def exchange(value):
    whole = value.reshape(ROWS * COLS, 1, -1)
    whole = lax.all_to_all(whole, ("gx", "gy"), 0, 0, tiled=True)
    return whole.reshape(value.shape)


def halo_x(low, high):
    return ring(high, "gx", 1), ring(low, "gx", -1)


def halo_y(current, xlo, xhi):
    first = jnp.concatenate([xlo[:, 1:, :2], current[:, :, :2], xhi[:, :1, :2]], axis=1)
    last = jnp.concatenate(
        [xlo[:, 1:, CY - 2 :], current[:, :, CY - 2 :], xhi[:, :1, CY - 2 :]], axis=1
    )
    return first, last


def ring(value, axis, steps):
    count = lax.axis_size(axis)
    return lax.ppermute(value, axis, [(i, (i + steps) % count) for i in range(count)])


def shards(farm_velocity, precursor_velocity, turb_cell, turb_slot, disk_mask):
    row = lax.axis_index("gx")
    column = lax.axis_index("gy")
    centre, face = (jnp.asarray(t) for t in vertical_tables())
    tables = jnp.asarray(plane_tables())
    order = (row * COLS + column).astype(F32)
    rise = (2.0 * jnp.sin(order * (math.pi / (2 * NZ)))).reshape(1, 1)
    with jax.named_scope("vertical_modes"):
        modes = pl.pallas_call(
            modes_kernel,
            out_shape=sds(3 * ROWS * COLS, CX * CY),
            in_specs=[pl.BlockSpec(memory_space=pltpu.HBM)] * 3,
            out_specs=VM,
            scratch_shapes=[
                pltpu.VMEM((3, CX, CY, NZ), F32),
                pltpu.VMEM((2, NZ, NZ), BF),
                pltpu.VMEM((2, NZ, NZ), BF),
                pltpu.SemaphoreType.DMA((5,)),
            ],
            compiler_params=pltpu.CompilerParams(vmem_limit_bytes=60 << 20),
        )(precursor_velocity, centre, face)
        modes, farm_velocity = lax.optimization_barrier((modes, farm_velocity))
        modes = exchange(modes)
    with jax.named_scope("farm_halo_y"):
        fylo = ring(farm_velocity[:, :, CY - 2 :], "gy", 1)
        fyhi = ring(farm_velocity[:, :, :2], "gy", -1)
    with jax.named_scope("planes"):
        modes = pl.pallas_call(
            plane_kernel,
            out_shape=sds(CHUNK * ROWS * COLS, CX * CY),
            in_specs=[SM] + [VM] * 2,
            out_specs=VM,
            compiler_params=LIMIT,
        )(rise, modes, tables)
        modes, fylo, fyhi = lax.optimization_barrier((modes, fylo, fyhi))
        modes = exchange(modes)
    with jax.named_scope("farm_halo_x"):
        low, high = (
            jnp.concatenate([fylo[:, part], farm_velocity[:, part], fyhi[:, part]], axis=2)
            for part in (slice(0, 2), slice(CX - 2, CX))
        )
        fxlo, fxhi = halo_x(low, high)
    cell = turb_cell.reshape(1, SLOTS)
    slot = jnp.where(disk_mask.reshape(1, SLOTS) == 1, turb_slot.reshape(1, SLOTS), -1)
    index = jnp.concatenate([cell // NZ, cell % NZ, slot, jnp.zeros((5, SLOTS), jnp.int32)], axis=0)
    with jax.named_scope("levels"):
        phys, state, xlo, xhi, ylo, yhi, force = pl.pallas_call(
            levels_kernel,
            out_shape=(sds(3, CX, CY, NZ),) * 2
            + (sds(3, 2, CY, NZ),) * 2
            + (sds(3, CX + 2, 2, NZ),) * 2
            + (sds(CX, CY, NZ),),
            in_specs=[SM] + [VM] * 9,
            out_specs=(VM,) * 7,
            scratch_shapes=[pltpu.VMEM((CX, CY, NZ), F32)],
            compiler_params=LIMIT,
        )(row.reshape(1).astype(jnp.int32), modes, farm_velocity, fxlo, fxhi, fylo, fyhi, centre, face, index)
    current = state
    weights = ((0.0, 1.0), (0.75, 0.25), (1.0 / 3.0, 2.0 / 3.0))
    for section, (alpha, beta) in enumerate(weights):
        with jax.named_scope("drag"):
            force = force if section == 0 else pl.pallas_call(
                force_kernel,
                grid=(1,),
                out_shape=sds(CX, CY, NZ),
                in_specs=[
                    pl.BlockSpec((None, CX, CY, NZ), lambda i: (0, 0, 0, 0)),
                    pl.BlockSpec((8, SLOTS), lambda i: (0, 0)),
                ],
                out_specs=pl.BlockSpec((CX, CY, NZ), lambda i: (0, 0, 0)),
                compiler_params=LIMIT,
                cost_estimate=cost(1),
            )(current, index)
        if section > 0:
            with jax.named_scope("halo"):
                xlo, xhi = halo_x(low, high)
                if section == 1:
                    phys, xlo, xhi = lax.optimization_barrier((phys, xlo, xhi))
                    precursor_new = lax.ppermute(phys, "gx", [(home(i), i) for i in range(ROWS)])
                first, last = halo_y(current, xlo, xhi)
                ylo, yhi = ring(last, "gy", 1), ring(first, "gy", -1)
        scratch = [
            pltpu.VMEM((3, CX + 4, EXT, LANES), F32),
            pltpu.VMEM((CX + 4, EXT, LANES), F32),
        ]
        operands = (current, xlo, xhi, ylo, yhi, state, force)
        if section == 2:
            with jax.named_scope("whole"):
                current, precursor_new = pl.pallas_call(
                    functools.partial(whole_kernel, alpha, beta),
                    out_shape=(sds(3, CX, CY, NZ),) * 2,
                    in_specs=[VM] * 7 + [pl.BlockSpec(memory_space=pl.ANY)],
                    out_specs=(pl.BlockSpec(memory_space=pl.ANY),) * 2,
                    scratch_shapes=scratch
                    + [
                        pltpu.VMEM((3, CX, CY, NZ), F32),
                        pltpu.SemaphoreType.DMA,
                        pltpu.SemaphoreType.DMA((CX // GROUP,)),
                    ],
                    compiler_params=LIMIT,
                    cost_estimate=cost(5),
                )(*operands, precursor_new)
            break
        with jax.named_scope("edge"):
            low, high = pl.pallas_call(
                functools.partial(edge_kernel, alpha, beta),
                out_shape=(sds(3, 2, CY, NZ),) * 2,
                in_specs=[VM] * 7,
                out_specs=(VM,) * 2,
                scratch_shapes=scratch,
                compiler_params=LIMIT,
                cost_estimate=cost(2),
            )(*operands)
        if section == 0:
            low, high, state = lax.optimization_barrier((low, high, state))
            operands = operands[:5] + (state, force)
        with jax.named_scope("inner"):
            current = pl.pallas_call(
                functools.partial(inner_kernel, alpha, beta),
                out_shape=sds(3, CX, CY, NZ),
                in_specs=[VM] * 9,
                out_specs=VM,
                scratch_shapes=scratch,
                compiler_params=LIMIT,
                cost_estimate=cost(4),
            )(*operands, low, high)
    return current, precursor_new


def solution(mesh):
    return jax.shard_map(
        shards,
        mesh=mesh,
        in_specs=(
            P(None, "gx", "gy", None),
            P(None, "gx", "gy", None),
            P("gx", "gy", None),
            P("gx", "gy", None),
            P("gx", "gy", None),
        ),
        out_specs=(P(None, "gx", "gy", None), P(None, "gx", "gy", None)),
        check_vma=False,
    )
```

```python
import functools
import math

import jax
import jax.numpy as jnp
import ml_dtypes
import numpy as np
from jax import lax
from jax.experimental import pallas as pl
from jax.experimental.pallas import tpu as pltpu
from jax.sharding import PartitionSpec as P

NF = 48
TURB = 16
WIND = 3.0
STEP = 0.1
SMAG = 0.0289
THRUST = 1.33
DIFFUSE = 0.05

CX, CY, NZ = 16, 8, 192
NX, NY = 256, 128
ROWS, COLS = 16, 16
SLOTS = 256
FRINGE = NF // CX
LANES = 256

BF = jnp.bfloat16
F32 = jnp.float32


def split(table):
    table = np.asarray(table, np.float64)
    high = table.astype(np.float32).astype(ml_dtypes.bfloat16)
    low = (table - high.astype(np.float64)).astype(np.float32).astype(ml_dtypes.bfloat16)
    return np.stack([high, low])


def vertical_tables():
    height = np.arange(NZ)[None, :]
    order = np.arange(NZ)[:, None]
    scale = np.where(order == 0, math.sqrt(1.0 / NZ), math.sqrt(2.0 / NZ))
    centre = scale * np.cos(math.pi / (2 * NZ) * (order * (2 * height + 1) % (4 * NZ)))
    keep = (height < NZ - 1) & (order > 0)
    face = math.sqrt(2.0 / NZ) * np.sin(math.pi / NZ * (order * (height + 1) % (2 * NZ))) * keep
    return split(centre), split(face)


def home(row):
    if row < FRINGE:
        return row + ROWS - FRINGE
    if row >= ROWS - FRINGE:
        return row - (ROWS - FRINGE)
    return row


def plane_tables():
    half = NX // 2
    angle = 2.0 * math.pi / NX * (np.arange(half)[:, None] * np.arange(NX)[None, :] % NX)
    forward_x = np.concatenate([np.cos(angle), -np.sin(angle)], axis=0)
    weight = np.where(np.arange(half) == 0, 1.0, 2.0)[:, None] / NX
    inverse_x = np.concatenate([np.cos(angle) * weight, -np.sin(angle) * weight], axis=0).T
    order = np.concatenate([np.arange(CX) + CX * home(row) for row in range(ROWS)])
    places = (CX * np.arange(ROWS)[:, None] + np.array([-2, -1, CX, CX + 1])[None, :]) % NX
    source = np.where(places < NF, NX - NF + places, 0)
    beside = inverse_x[np.repeat(source.reshape(-1), 4)]
    inverse_x = inverse_x[order]
    angle = 2.0 * math.pi / NY * (np.arange(NY)[:, None] * np.arange(NY)[None, :] % NY)
    keep = (np.arange(NY) != NY // 2)[None, :]
    forward_y = np.concatenate([np.cos(angle) * keep, np.sin(angle) * keep], axis=1)
    inverse_y = np.concatenate([np.cos(angle), np.sin(angle)], axis=1) / NY
    return split(np.concatenate([forward_x, inverse_x, beside, forward_y, inverse_y], axis=0))


def halves(x):
    high = x.astype(BF)
    low = (x - high.astype(F32)).astype(BF)
    return high, low


def thirds(x):
    high, rest = x.astype(BF), x
    rest = rest - high.astype(F32)
    middle = rest.astype(BF)
    rest = rest - middle.astype(F32)
    return rest.astype(BF), middle, high


def dot3(a, b, dims):
    one = functools.partial(lax.dot_general, dimension_numbers=(dims, ((), ())), preferred_element_type=F32)
    return one(a[0], b[0]) + (one(a[0], b[1]) + one(a[1], b[0]))


NN = ((1,), (0,))
NT = ((1,), (1,))
TN = ((0,), (0,))


def modes_kernel(field_hbm, centre_hbm, face_hbm, out, field, centre, face, done):
    quarter = CX // 4
    pieces = [(centre_hbm.at[part], centre.at[part]) for part in range(2)]
    for c in range(3):
        if c == 2:
            pieces += [(face_hbm.at[part], face.at[part]) for part in range(2)]
        for first in range(0, CX, quarter):
            planes = slice(first, first + quarter)
            pieces.append((field_hbm.at[c, planes], field.at[c, planes]))
    copies = [
        pltpu.make_async_copy(source, target, done.at[i]) for i, (source, target) in enumerate(pieces)
    ]
    for copy in copies:
        copy.start()
    out[3 * NZ :, :] = jnp.zeros((3 * (ROWS * COLS - NZ), CX * CY), F32)
    for c, ready in ((0, copies[:6]), (1, copies[6:10]), (2, copies[10:])):
        for copy in ready:
            copy.wait()
        table = face if c == 2 else centre
        x = field[c].reshape(CX * CY, NZ)
        out[pl.ds(c, NZ, stride=3), :] = dot3((table[0], table[1]), halves(x), NT)


def swap_masks():
    row = lax.broadcasted_iota(jnp.int32, (8, CX * CY), 0)
    lane = lax.broadcasted_iota(jnp.int32, (8, CX * CY), 1)
    masks = []
    for bit in range(3):
        row_bit = (row >> bit) & 1
        lane_bit = (lane >> (3 + bit)) & 1
        masks.append(((row_bit < lane_bit), (row_bit > lane_bit), row_bit == 0))
    return masks, lane >= 64


def swapped(parts, masks):
    masks, upper = masks
    low, high = parts
    low, high = (
        jnp.where(upper, pltpu.roll(high, 64, 1), low),
        jnp.where(upper, high, pltpu.roll(low, 64, 1)),
    )
    out = []
    for x in (low, high):
        for bit in range(3):
            later, earlier, even = masks[bit]
            by_row, by_lane = 1 << bit, 8 << bit
            other = pltpu.roll(x, by_row, 0)
            if by_row != 4:
                other = jnp.where(even, pltpu.roll(x, 8 - by_row, 0), other)
            x = jnp.where(
                later,
                pltpu.roll(other, by_lane, 1),
                jnp.where(earlier, pltpu.roll(other, CX * CY - by_lane, 1), x),
            )
        out.append(x)
    return out


CHUNK = 6


def halo_slots(own, near):
    part = lax.broadcasted_iota(jnp.int32, own.shape, 0) % 4
    slot = lax.broadcasted_iota(jnp.int32, own.shape, 1) % 8
    across = jnp.where(slot < 2, pltpu.roll(own, 2, 1), pltpu.roll(own, 122, 1))
    corner = jnp.where(slot < 6, pltpu.roll(near, 6, 1), pltpu.roll(near, 126, 1))
    along = jnp.where(part == 0, pltpu.roll(near, 4, 1), jnp.where(part == 1, near, corner))
    return jnp.where(slot < 4, across, along)


def plane_kernel(rise_ref, inp, tables, out):
    bounds = (0, NX, 2 * NX, 3 * NX, 3 * NX + NY, 3 * NX + 2 * NY)
    fx, ix, ix2, fy, iy = (
        tuple(tables[part, bounds[i] : bounds[i + 1]] for part in range(2)) for i in range(5)
    )
    half = NX // 2
    masks = swap_masks()
    spec = []
    for c in range(3):
        rows = []
        for r in range(2 * ROWS):
            rows.append(inp[pl.ds(24 * r + c, 8, stride=3), :])
            if r % 2 == 1:
                rows[-2:] = swapped(rows[-2:], masks)
        x = jnp.concatenate(rows, axis=0)
        along = dot3((fx[0], fx[1]), halves(x), NN)
        both = dot3(halves(along), (fy[0], fy[1]), NN)
        re = both[:half, :NY] + both[half:, NY:]
        im = both[half:, :NY] - both[:half, NY:]
        spec.append((re, im))
    rise = rise_ref[0, 0]
    k = lax.broadcasted_iota(jnp.int32, (half, NY), 0)
    q = lax.broadcasted_iota(jnp.int32, (half, NY), 1)
    kx = (2.0 * math.pi / NX) * k.astype(F32)
    ky = (2.0 * math.pi / NY) * jnp.where(q < NY // 2, q, q - NY).astype(F32)
    hor = kx * kx + ky * ky
    bound = hor + rise * rise
    inverse = jnp.where(bound > 0.0, -1.0 / jnp.where(bound > 0.0, bound, 1.0), 0.0)
    decay = jnp.exp(-DIFFUSE * hor)
    (ur, ui), (vr, vi), (wr, wi) = spec
    press_re = (rise * wr - kx * ui - ky * vi) * inverse
    press_im = (rise * wi + kx * ur + ky * vr) * inverse
    new = (
        ((ur + kx * press_im) * decay, (ui - kx * press_re) * decay),
        ((vr + ky * press_im) * decay, (vi - ky * press_re) * decay),
        ((wr + rise * press_re) * decay, (wi + rise * press_im) * decay),
    )
    for c in range(3):
        both = dot3(halves(jnp.concatenate(new[c], axis=0)), (iy[0], iy[1]), NN)
        re = both[:half, :NY] - both[half:, NY:]
        im = both[:half, NY:] + both[half:, :NY]
        lines = halves(jnp.concatenate([re, im], axis=0))
        x = dot3((ix[0], ix[1]), lines, NN)
        near = dot3((ix2[0], ix2[1]), lines, NN)
        for r in range(ROWS):
            here = [slice(16 * r + 8 * side, 16 * r + 8 * side + 8) for side in range(2)]
            own = [x[rows] for rows in here]
            pair = swapped(own, masks)
            halo = swapped([halo_slots(own[side], near[here[side]]) for side in range(2)], masks)
            for side in range(2):
                first = CHUNK * (16 * r + 8 * side)
                out[pl.ds(first + c, 8, stride=CHUNK), :] = pair[side]
                out[pl.ds(first + 3 + c, 8, stride=CHUNK), :] = halo[side]


def levels_kernel(
    row_ref, modes, farm, fxlo, fxhi, fylo, fyhi, centre, face, index,
    phys, state, xlo, xhi, ylo, yhi, force, q,
):
    row = row_ref[0]
    fringe = row < FRINGE
    below = (row >= 1) & (row <= FRINGE)
    above = (row < FRINGE - 1) | (row == ROWS - 1)
    for c in range(3):
        table = face if c == 2 else centre
        x = modes[pl.ds(c, NZ, stride=CHUNK), :]
        y = dot3(halves(x), (table[0], table[1]), TN).reshape(CX, CY, NZ)
        phys[c] = y
        state[c] = jnp.where(fringe, y, farm[c])
        if c == 0:
            force[...] = slot_force(state[0].reshape(CX * CY, NZ), index).reshape(CX, CY, NZ)
        x = modes[pl.ds(3 + c, NZ, stride=CHUNK), :]
        q[...] = dot3(halves(x), (table[0], table[1]), TN).reshape(CX, CY, NZ)
        ylo[c, 1 : CX + 1] = jnp.where(fringe, q[:, 0:2], fylo[c])
        yhi[c, 1 : CX + 1] = jnp.where(fringe, q[:, 2:4], fyhi[c])
        ylo[c, 0] = jnp.where(below, q[6, 4:6], fxlo[c, 1, 0:2])
        yhi[c, 0] = jnp.where(below, q[6, 6:8], fxlo[c, 1, CY + 2 :])
        ylo[c, CX + 1] = jnp.where(above, q[10, 4:6], fxhi[c, 0, 0:2])
        yhi[c, CX + 1] = jnp.where(above, q[10, 6:8], fxhi[c, 0, CY + 2 :])
        for i in range(2):
            for half in range(2):
                lines = slice(4 * half, 4 * half + 4)
                wide = slice(4 * half + 2, 4 * half + 6)
                xlo[c, i, lines] = jnp.where(below, q[4 * i + half, 4:8], fxlo[c, i, wide])
                xhi[c, i, lines] = jnp.where(above, q[8 + 4 * i + half, 4:8], fxhi[c, i, wide])


def slot_force(u, index):
    column = index[0:1, :]
    level = index[1:2, :]
    turbine = index[2:3, :]
    at_column = jnp.where(
        lax.broadcasted_iota(jnp.int32, (CX * CY, SLOTS), 0) == column, 1.0, 0.0
    ).astype(BF)
    at_level = lax.broadcasted_iota(jnp.int32, (NZ, SLOTS), 0) == level
    owned = jnp.where(lax.broadcasted_iota(jnp.int32, (TURB, SLOTS), 0) == turbine, 1.0, 0.0)
    one = functools.partial(lax.dot_general, preferred_element_type=F32)
    picked = sum(one(part, at_column, dimension_numbers=(TN, ((), ()))) for part in thirds(u))
    values = jnp.sum(jnp.where(at_level, picked, 0.0), axis=0, keepdims=True) + WIND
    sums = jnp.sum(owned * values, axis=1, keepdims=True)
    counts = jnp.sum(owned, axis=1, keepdims=True)
    mean = sums / jnp.maximum(counts, 1.0)
    thrust = -0.5 * THRUST * mean * jnp.abs(mean)
    per_slot = jnp.sum(owned * thrust, axis=0, keepdims=True)
    parts = thirds(jnp.where(at_level, per_slot, 0.0))
    return sum(one(at_column, part, dimension_numbers=(NT, ((), ()))) for part in parts)


EXT = 16
OFF = 4
DIAGONAL = 0.5 * SMAG * SMAG
CROSS = 0.25 * SMAG * SMAG


def force_kernel(cur, index, force):
    force[...] = slot_force(cur[...].reshape(CX * CY, NZ), index).reshape(CX, CY, NZ)


def after_y(x):
    return pltpu.roll(x, EXT - 1, 0)


def before_y(x):
    return pltpu.roll(x, 1, 0)


def after_z(x):
    return pltpu.roll(x, LANES - 1, 1)


def before_z(x):
    return pltpu.roll(x, 1, 1)


def assemble(s, cur, xlo, xhi, ylo, yhi, begin, end):
    for c in range(3):
        s[c, begin:end] = jnp.zeros((end - begin, EXT, LANES), F32)
        own = slice(max(begin, 2), min(end, CX + 2))
        s[c, own, OFF : OFF + CY, :NZ] = cur[c, own.start - 2 : own.stop - 2]
        if begin < 2:
            s[c, begin:2, OFF : OFF + CY, :NZ] = xlo[c, begin:2]
        if end > CX + 2:
            s[c, CX + 2 : end, OFF : OFF + CY, :NZ] = xhi[c, : end - CX - 2]
        near = slice(max(begin, 1), min(end, CX + 3))
        s[c, near, OFF - 2 : OFF, :NZ] = ylo[c, near.start - 1 : near.stop - 1]
        s[c, near, OFF + CY : OFF + CY + 2, :NZ] = yhi[c, near.start - 1 : near.stop - 1]


def viscosity(s, e, p):
    f = [s[c, p] for c in range(3)]
    dx = [s[c, p + 1] - s[c, p - 1] for c in range(3)]
    dy = [after_y(f[c]) - before_y(f[c]) for c in range(3)]
    dz = [after_z(f[c]) - before_z(f[c]) for c in range(3)]
    uv = dy[0] + dx[1]
    uw = dz[0] + dx[2]
    vw = dz[1] + dy[2]
    e[p] = jnp.sqrt(
        DIAGONAL * (dx[0] * dx[0] + dy[1] * dy[1] + dz[2] * dz[2])
        + CROSS * (uv * uv + uw * uw + vw * vw)
    )


def fluxes(speed, eddy, fa, fb):
    speed = 0.25 * speed
    eddy = 0.5 * eddy
    plus = speed + eddy
    minus = speed - eddy
    return [plus * fa[c] + minus * fb[c] for c in range(3)]


def face(s, e, p):
    own = slice(OFF, OFF + CY)
    fa = [s[c, p, own, :] for c in range(3)]
    fb = [s[c, p + 1, own, :] for c in range(3)]
    return fluxes(fa[0] + fb[0] + 2.0 * WIND, e[p, own, :] + e[p + 1, own, :], fa, fb)


def advance(alpha, beta, s, e, force, base, store, p, below):
    own, later, earlier = (slice(OFF + step, OFF + step + CY) for step in (0, 1, -1))
    f = [s[c, p, own, :] for c in range(3)]
    eddy = e[p, own, :]
    above = face(s, e, p)
    fy = [s[c, p, later, :] for c in range(3)]
    left_y = fluxes(f[1] + fy[1], eddy + e[p, later, :], f, fy)
    fy = [s[c, p, earlier, :] for c in range(3)]
    right_y = fluxes(f[1] + fy[1], eddy + e[p, earlier, :], fy, f)
    fz = [after_z(f[c]) for c in range(3)]
    along_z = fluxes(f[2] + fz[2], eddy + after_z(eddy), f, fz)
    for c in range(3):
        rate = (
            (below[c] - above[c])
            + (right_y[c] - left_y[c])
            + (before_z(along_z[c]) - along_z[c])
        )
        value = (beta * (f[c] + STEP * rate))[:, :NZ]
        if c == 0:
            value = value + (beta * STEP) * force[p - 2]
        if alpha != 0.0:
            value = value + alpha * base[c, p - 2]
        store(c, p - 2, value)
    return above


def edge_kernel(alpha, beta, cur, xlo, xhi, ylo, yhi, base, force, low, high, s, e):
    assemble(s, cur, xlo, xhi, ylo, yhi, 0, 6)
    assemble(s, cur, xlo, xhi, ylo, yhi, CX - 2, CX + 4)
    for start, out in ((2, low), (CX, high)):
        for p in range(start - 1, start + 3):
            viscosity(s, e, p)

        def store(c, x, value, out=out, start=start):
            out[c, x + 2 - start] = value

        below = face(s, e, start - 1)
        for p in (start, start + 1):
            below = advance(alpha, beta, s, e, force, base, store, p, below)


GROUP = 4


def whole_kernel(
    alpha, beta, cur, xlo, xhi, ylo, yhi, base, force, other, out, kept, s, e, new, done, sent
):
    copies = [pltpu.make_async_copy(other, kept, done)]
    copies[0].start()
    assemble(s, cur, xlo, xhi, ylo, yhi, 0, CX + 4)

    for p in range(1, CX + 3):
        viscosity(s, e, p)

    def store(c, x, value):
        new[c, x] = value

    below = face(s, e, 1)
    for p in range(2, CX + 2):
        below = advance(alpha, beta, s, e, force, base, store, p, below)
        if (p - 1) % GROUP == 0:
            planes = slice(p - 1 - GROUP, p - 1)
            copies.append(
                pltpu.make_async_copy(new.at[:, planes], out.at[:, planes], sent.at[p // GROUP - 1])
            )
            copies[-1].start()
    for copy in copies:
        copy.wait()


def inner_kernel(alpha, beta, cur, xlo, xhi, ylo, yhi, base, force, low, high, new, s, e):
    assemble(s, cur, xlo, xhi, ylo, yhi, 2, CX + 2)

    for p in range(3, CX + 1):
        viscosity(s, e, p)

    def store(c, x, value):
        new[c, x] = value

    below = face(s, e, 3)
    for p in range(4, CX):
        below = advance(alpha, beta, s, e, force, base, store, p, below)
    for c in range(3):
        new[c, :2] = low[c]
        new[c, CX - 2 :] = high[c]


def sds(*shape):
    return jax.ShapeDtypeStruct(shape, F32)


def cost(micros):
    return pl.CostEstimate(flops=1000000 * micros, bytes_accessed=3000000 * micros, transcendentals=0)


VM = pl.BlockSpec(memory_space=pltpu.VMEM)
SM = pl.BlockSpec(memory_space=pltpu.SMEM)
LIMIT = pltpu.CompilerParams(vmem_limit_bytes=48 << 20)


def exchange(value):
    whole = value.reshape(ROWS * COLS, 1, -1)
    whole = lax.all_to_all(whole, ("gx", "gy"), 0, 0, tiled=True)
    return whole.reshape(value.shape)


def halo_x(low, high):
    return ring(high, "gx", 1), ring(low, "gx", -1)


def halo_y(current, xlo, xhi):
    first = jnp.concatenate([xlo[:, 1:, :2], current[:, :, :2], xhi[:, :1, :2]], axis=1)
    last = jnp.concatenate(
        [xlo[:, 1:, CY - 2 :], current[:, :, CY - 2 :], xhi[:, :1, CY - 2 :]], axis=1
    )
    return first, last


def ring(value, axis, steps):
    count = lax.axis_size(axis)
    return lax.ppermute(value, axis, [(i, (i + steps) % count) for i in range(count)])


def shards(farm_velocity, precursor_velocity, turb_cell, turb_slot, disk_mask):
    row = lax.axis_index("gx")
    column = lax.axis_index("gy")
    centre, face = (jnp.asarray(t) for t in vertical_tables())
    tables = jnp.asarray(plane_tables())
    order = (row * COLS + column).astype(F32)
    rise = (2.0 * jnp.sin(order * (math.pi / (2 * NZ)))).reshape(1, 1)
    with jax.named_scope("vertical_modes"):
        modes = pl.pallas_call(
            modes_kernel,
            out_shape=sds(3 * ROWS * COLS, CX * CY),
            in_specs=[pl.BlockSpec(memory_space=pltpu.HBM)] * 3,
            out_specs=VM,
            scratch_shapes=[
                pltpu.VMEM((3, CX, CY, NZ), F32),
                pltpu.VMEM((2, NZ, NZ), BF),
                pltpu.VMEM((2, NZ, NZ), BF),
                pltpu.SemaphoreType.DMA((16,)),
            ],
            compiler_params=pltpu.CompilerParams(vmem_limit_bytes=60 << 20),
        )(precursor_velocity, centre, face)
        modes, farm_velocity = lax.optimization_barrier((modes, farm_velocity))
        modes = exchange(modes)
    with jax.named_scope("farm_halo_y"):
        fylo = ring(farm_velocity[:, :, CY - 2 :], "gy", 1)
        fyhi = ring(farm_velocity[:, :, :2], "gy", -1)
    with jax.named_scope("planes"):
        modes = pl.pallas_call(
            plane_kernel,
            out_shape=sds(CHUNK * ROWS * COLS, CX * CY),
            in_specs=[SM] + [VM] * 2,
            out_specs=VM,
            compiler_params=LIMIT,
        )(rise, modes, tables)
        modes, fylo, fyhi = lax.optimization_barrier((modes, fylo, fyhi))
        modes = exchange(modes)
    with jax.named_scope("farm_halo_x"):
        low, high = (
            jnp.concatenate([fylo[:, part], farm_velocity[:, part], fyhi[:, part]], axis=2)
            for part in (slice(0, 2), slice(CX - 2, CX))
        )
        fxlo, fxhi = halo_x(low, high)
    cell = turb_cell.reshape(1, SLOTS)
    slot = jnp.where(disk_mask.reshape(1, SLOTS) == 1, turb_slot.reshape(1, SLOTS), -1)
    index = jnp.concatenate([cell // NZ, cell % NZ, slot, jnp.zeros((5, SLOTS), jnp.int32)], axis=0)
    with jax.named_scope("levels"):
        phys, state, xlo, xhi, ylo, yhi, force = pl.pallas_call(
            levels_kernel,
            out_shape=(sds(3, CX, CY, NZ),) * 2
            + (sds(3, 2, CY, NZ),) * 2
            + (sds(3, CX + 2, 2, NZ),) * 2
            + (sds(CX, CY, NZ),),
            in_specs=[SM] + [VM] * 9,
            out_specs=(VM,) * 7,
            scratch_shapes=[pltpu.VMEM((CX, CY, NZ), F32)],
            compiler_params=LIMIT,
        )(row.reshape(1).astype(jnp.int32), modes, farm_velocity, fxlo, fxhi, fylo, fyhi, centre, face, index)
    current = state
    weights = ((0.0, 1.0), (0.75, 0.25), (1.0 / 3.0, 2.0 / 3.0))
    for section, (alpha, beta) in enumerate(weights):
        with jax.named_scope("drag"):
            force = force if section == 0 else pl.pallas_call(
                force_kernel,
                grid=(1,),
                out_shape=sds(CX, CY, NZ),
                in_specs=[
                    pl.BlockSpec((None, CX, CY, NZ), lambda i: (0, 0, 0, 0)),
                    pl.BlockSpec((8, SLOTS), lambda i: (0, 0)),
                ],
                out_specs=pl.BlockSpec((CX, CY, NZ), lambda i: (0, 0, 0)),
                compiler_params=LIMIT,
                cost_estimate=cost(1),
            )(current, index)
        if section > 0:
            with jax.named_scope("halo"):
                xlo, xhi = halo_x(low, high)
                if section == 1:
                    phys, xlo, xhi = lax.optimization_barrier((phys, xlo, xhi))
                    precursor_new = lax.ppermute(phys, "gx", [(home(i), i) for i in range(ROWS)])
                first, last = halo_y(current, xlo, xhi)
                ylo, yhi = ring(last, "gy", 1), ring(first, "gy", -1)
        scratch = [
            pltpu.VMEM((3, CX + 4, EXT, LANES), F32),
            pltpu.VMEM((CX + 4, EXT, LANES), F32),
        ]
        operands = (current, xlo, xhi, ylo, yhi, state, force)
        if section == 2:
            with jax.named_scope("whole"):
                current, precursor_new = pl.pallas_call(
                    functools.partial(whole_kernel, alpha, beta),
                    out_shape=(sds(3, CX, CY, NZ),) * 2,
                    in_specs=[VM] * 7 + [pl.BlockSpec(memory_space=pl.ANY)],
                    out_specs=(pl.BlockSpec(memory_space=pl.ANY),) * 2,
                    scratch_shapes=scratch
                    + [
                        pltpu.VMEM((3, CX, CY, NZ), F32),
                        pltpu.SemaphoreType.DMA,
                        pltpu.SemaphoreType.DMA((CX // GROUP,)),
                    ],
                    compiler_params=LIMIT,
                    cost_estimate=cost(5),
                )(*operands, precursor_new)
            break
        with jax.named_scope("edge"):
            low, high = pl.pallas_call(
                functools.partial(edge_kernel, alpha, beta),
                out_shape=(sds(3, 2, CY, NZ),) * 2,
                in_specs=[VM] * 7,
                out_specs=(VM,) * 2,
                scratch_shapes=scratch,
                compiler_params=LIMIT,
                cost_estimate=cost(2),
            )(*operands)
        if section == 0:
            low, high, state = lax.optimization_barrier((low, high, state))
            operands = operands[:5] + (state, force)
        with jax.named_scope("inner"):
            current = pl.pallas_call(
                functools.partial(inner_kernel, alpha, beta),
                out_shape=sds(3, CX, CY, NZ),
                in_specs=[VM] * 9,
                out_specs=VM,
                scratch_shapes=scratch,
                compiler_params=LIMIT,
                cost_estimate=cost(4),
            )(*operands, low, high)
    return current, precursor_new


def solution(mesh):
    return jax.shard_map(
        shards,
        mesh=mesh,
        in_specs=(
            P(None, "gx", "gy", None),
            P(None, "gx", "gy", None),
            P("gx", "gy", None),
            P("gx", "gy", None),
            P("gx", "gy", None),
        ),
        out_specs=(P(None, "gx", "gy", None), P(None, "gx", "gy", None)),
        check_vma=False,
    )
```
